128 devices in a mesh: frames: 4 (over z_lo, core), rows: 32 (over z_hi, y, x).
Axes of the slice: x: 4, y: 4, z: 4 (z_hi: 2, z_lo: 2; z = z_hi * 2 + z_lo), core: 2. Of those that a mesh axis runs over, the one named last changes fastest.
Arguments:
- clip_in: bfloat16 [16, 128, 64, 256], P('frames', 'rows'), may hold values from -6 to 6
- kernel_one: bfloat16 [3, 3, 3, 64, 64], replicated, may hold values from -0.15625 to 0.15625
- bias_one: float32 [64], replicated, may hold values from -3 to 3
- kernel_two: bfloat16 [3, 3, 3, 64, 64], replicated, may hold values from -0.3125 to 0.3125
- cotangent: bfloat16 [16, 128, 64, 256], P('frames', 'rows'), may hold values from -6 to 6
Outputs:
- block_out: bfloat16 [16, 128, 64, 256], P('frames', 'rows')
- grad_input: bfloat16 [16, 128, 64, 256], P('frames', 'rows')
- grad_first: float32 [3, 3, 3, 64, 64], replicated
- grad_second: float32 [3, 3, 3, 64, 64], replicated
- grad_bias: float32 [64], replicated
The draws below stay inside these ranges and needn't reach their ends.
All inputs are finite; a program needn't handle non-finite values.
Results may differ from the reference program's by a relative error of at most 0.0065.
Values may be sent and summed in bfloat16 or wider, within the bound.
No kernel may reach another device: no remote copies, remote signals or barrier semaphores. Data moves between devices by JAX's collectives and lax.ppermute only.
A program may use at most 64 MiB of HBM per device.

```python
import math
import jax
import jax.numpy as jnp
from jax import lax

C = 64
COLS = 256
FRAMES = 16
ROWS = 128


def shard_levels(key, shape, cuts, low, largest):
    gain = 1.0
    for dim, blocks in cuts:
        heights = jax.random.uniform(jax.random.fold_in(jax.random.fold_in(key, 6), dim), (blocks,), jnp.float32, low / len(cuts), largest / len(cuts))
        gain = gain * jnp.repeat(jnp.exp(heights), shape[dim] // blocks).reshape((-1,) + (1,) * (len(shape) - 1 - dim))
    return gain


def normal_values(own_key, dims, spread, most, split=(), kind=jnp.bfloat16):
    gain = shard_levels(own_key, dims, split, -0.22, 0.18) if split else 1.0
    array = jax.random.normal(own_key, dims, jnp.float32) * spread * gain
    return jnp.minimum(jnp.maximum(array, -most), most).astype(kind)


def setup_inputs(seed: int = 0) -> dict:
    streams_of = jax.random.split(jax.random.key(seed), 6)
    clip_in = normal_values(streams_of[0], (FRAMES, ROWS, C, COLS), 1.0, 6.0, ((0, 4), (1, 32)))
    kernel_one = normal_values(streams_of[1], (3, 3, 3, C, C), (27 * C) ** -0.5, 0.15625)
    bias_one = normal_values(streams_of[2], (C,), 0.5, 3.0, (), jnp.float32)
    kernel_two = normal_values(streams_of[3], (3, 3, 3, C, C), (27 * C // 4) ** -0.5, 0.3125)
    cotangent = normal_values(streams_of[4], (FRAMES, ROWS, C, COLS), 1.0, 6.0, ((0, 4), (1, 32)))
    return dict(clip_in=clip_in, kernel_one=kernel_one, bias_one=bias_one, kernel_two=kernel_two, cotangent=cotangent)


def conv(field, kernel):
    lhs = jnp.transpose(field.astype(jnp.float32), (2, 0, 1, 3))[None]
    rhs = jnp.transpose(kernel.astype(jnp.float32), (3, 4, 0, 1, 2))
    result = lax.conv_general_dilated(lhs, rhs, (1, 1, 1), [(2, 0), (1, 1), (1, 1)], dimension_numbers=('NCDHW', 'OIDHW', 'NCDHW'), precision=lax.Precision.HIGHEST)
    return jnp.transpose(result[0], (1, 2, 0, 3))

def reference(clip_in, kernel_one, bias_one, kernel_two, cotangent):
    hidden = conv(clip_in, kernel_one) + bias_one.astype(jnp.float32)[None, None, :, None]
    active = jax.nn.silu(hidden).astype(jnp.bfloat16)
    block_out = (clip_in.astype(jnp.float32) + conv(active, kernel_two)).astype(jnp.bfloat16)
    unused_two, pull_two = jax.vjp(conv, active.astype(jnp.float32), kernel_two.astype(jnp.float32))
    grad_act, grad_second = pull_two(cotangent.astype(jnp.float32))
    sig = jax.nn.sigmoid(hidden)
    grad_pre = (grad_act * sig * (1.0 + hidden * (1.0 - sig))).astype(jnp.bfloat16)
    unused_one, pull_one = jax.vjp(conv, clip_in.astype(jnp.float32), kernel_one.astype(jnp.float32))
    grad_back, grad_first = pull_one(grad_pre.astype(jnp.float32))
    grad_input = (cotangent.astype(jnp.float32) + grad_back).astype(jnp.bfloat16)
    inv_scale = 1.0 / math.sqrt(FRAMES * ROWS * COLS)
    grad_bias = lax.optimization_barrier(jnp.sum(grad_pre.astype(jnp.float32), axis=(0, 1, 3))) * inv_scale
    return (block_out, grad_input, grad_first * inv_scale, grad_second * inv_scale, grad_bias)
```

```python
import math

import jax
import jax.numpy as jnp
from jax import lax
from jax.sharding import PartitionSpec as P

AXES = ("frames", "rows")


def pairs_of(count, first):
    pairs = []
    for i in range(first, count - 1, 2):
        pairs += [(i, i + 1), (i + 1, i)]
    return pairs


def swap_neighbours(axis, to_next, to_prior):
    count = lax.axis_size(axis)
    even = lax.axis_index(axis) % 2 == 0
    odd_pairs = lax.ppermute(jnp.where(even, to_prior, to_next), axis, pairs_of(count, 1))
    even_pairs = lax.ppermute(jnp.where(even, to_next, to_prior), axis, pairs_of(count, 0))
    return jnp.where(even, odd_pairs, even_pairs), jnp.where(even, even_pairs, odd_pairs)


def extend(past, future):
    both = jnp.stack([past, future])
    low, high = swap_neighbours("rows", both[:, :, -1:], both[:, :, :1])
    past_rows, future_rows = jnp.concatenate([low, both, high], axis=2)
    earlier, later = swap_neighbours("frames", past_rows[-2:], future_rows[:2])
    return (
        jnp.concatenate([earlier, past_rows], axis=0),
        jnp.concatenate([future_rows, later], axis=0),
    )


def spatial_taps(extended, row_count, col_count, flipped):
    padded = jnp.pad(extended, ((0, 0), (0, 0), (0, 0), (1, 1)))
    pieces = []
    for i in range(3):
        for j in range(3):
            row_start = 2 - i if flipped else i
            col_start = 2 - j if flipped else j
            pieces.append(
                padded[:, row_start : row_start + row_count, :, col_start : col_start + col_count]
            )
    return jnp.concatenate(pieces, axis=2)


def forward_conv(taps, kernel, frame_count):
    running = None
    for t in range(3):
        flat_kernel = jnp.transpose(kernel[t], (2, 0, 1, 3)).reshape((kernel.shape[3], -1))
        term = jnp.einsum(
            "ok,frkw->frow",
            flat_kernel,
            taps[t : t + frame_count],
            preferred_element_type=jnp.float32,
        )
        running = term if running is None else running + term
    return running


def adjoint_conv(taps, kernel, frame_count):
    running = None
    for t in range(3):
        flat_kernel = jnp.transpose(kernel[t], (3, 0, 1, 2)).reshape((kernel.shape[4], -1))
        term = jnp.einsum(
            "ck,frkw->frcw",
            flat_kernel,
            taps[2 - t : 2 - t + frame_count],
            preferred_element_type=jnp.float32,
        )
        running = term if running is None else running + term
    return running


def total_over_devices(value):
    count = lax.axis_size("frames") * lax.axis_size("rows")
    parts = value.astype(jnp.bfloat16).reshape((count, 16, 128))
    mine = lax.all_to_all(parts, AXES, 0, 0, tiled=True)
    mine = jnp.sum(mine.astype(jnp.float32), axis=0).astype(jnp.bfloat16)
    spread = jnp.broadcast_to(mine[None], parts.shape)
    return lax.all_to_all(spread, AXES, 0, 0, tiled=True).reshape(value.shape).astype(jnp.float32)


def per_device(clip_in, kernel_one, bias_one, kernel_two, cotangent):
    frame_count, row_count, channels, col_count = clip_in.shape
    devices = lax.axis_size("frames") * lax.axis_size("rows")
    input_ext, cot_ext = extend(clip_in, cotangent)
    input_taps = spatial_taps(input_ext, row_count, col_count, False)
    cot_taps = spatial_taps(cot_ext, row_count, col_count, True)
    hidden = forward_conv(input_taps, kernel_one, frame_count) + bias_one[None, None, :, None]
    active = jax.nn.silu(hidden).astype(jnp.bfloat16)
    grad_act = adjoint_conv(cot_taps, kernel_two, frame_count)
    sig = jax.nn.sigmoid(hidden)
    grad_pre = (grad_act * sig * (1.0 + hidden * (1.0 - sig))).astype(jnp.bfloat16)

    first, second = [], []
    for t in range(3):
        part = jnp.einsum(
            "frow,frkw->ok",
            grad_pre,
            input_taps[t : t + frame_count],
            preferred_element_type=jnp.float32,
        )
        first.append(jnp.transpose(part.reshape((channels, 9, channels)), (1, 0, 2)))
        part = jnp.einsum(
            "frkw,frcw->kc",
            cot_taps[2 - t : 2 - t + frame_count],
            active,
            preferred_element_type=jnp.float32,
        )
        second.append(part.reshape((9, channels, channels)))
    bias = jnp.sum(grad_pre.astype(jnp.float32), axis=(0, 1, 3))
    terms = jnp.concatenate([jnp.stack(first), jnp.stack(second)], axis=3)
    terms = terms.reshape((-1, 2 * channels))
    tail = jnp.zeros((devices * 16 - terms.shape[0], 2 * channels), jnp.float32)
    tail = tail.at[0, :channels].set(bias)
    total = total_over_devices(jnp.concatenate([terms, tail], axis=0))

    active_ext, pre_ext = extend(active, grad_pre)
    active_taps = spatial_taps(active_ext, row_count, col_count, False)
    pre_taps = spatial_taps(pre_ext, row_count, col_count, True)
    block_out = (
        clip_in.astype(jnp.float32) + forward_conv(active_taps, kernel_two, frame_count)
    ).astype(jnp.bfloat16)
    grad_back = adjoint_conv(pre_taps, kernel_one, frame_count)
    grad_input = (cotangent.astype(jnp.float32) + grad_back).astype(jnp.bfloat16)

    cell_total = (
        frame_count * lax.axis_size("frames") * row_count * lax.axis_size("rows") * col_count
    )
    total = total * (1.0 / math.sqrt(cell_total))
    count = terms.shape[0]
    return (
        block_out,
        grad_input,
        total[:count, :channels].reshape(kernel_one.shape),
        total[:count, channels:].reshape(kernel_two.shape),
        total[count, :channels],
    )


def solution(mesh):
    in_specs = (P("frames", "rows", None, None), P(), P(), P(), P("frames", "rows", None, None))
    out_specs = (P("frames", "rows", None, None), P("frames", "rows", None, None), P(), P(), P())
    return jax.shard_map(
        per_device, mesh=mesh, in_specs=in_specs, out_specs=out_specs, check_vma=False
    )
```

```python
import math

import jax
import jax.numpy as jnp
from jax import lax
from jax.experimental import pallas as pl
from jax.experimental.pallas import tpu as pltpu
from jax.sharding import PartitionSpec as P

F32, BF16 = jnp.float32, jnp.bfloat16


def put_taps(dst, g, rr, slab):
    chan, cols = slab.shape
    lane = lax.broadcasted_iota(jnp.int32, slab.shape, 1)
    zero = jnp.zeros_like(slab)
    dst[g, rr, 0:chan, :] = jnp.where(lane == 0, zero, pltpu.roll(slab, 1, 1))
    dst[g, rr, chan : 2 * chan, :] = slab
    dst[g, rr, 2 * chan : 3 * chan, :] = jnp.where(lane == cols - 1, zero, pltpu.roll(slab, cols - 1, 1))


def build(side, past, future, rows_odd, rows_even, main_odd, main_even, rim_odd, rim_even, xp, xf):
    frames, rows = past.shape[0], past.shape[1]
    row_even, frame_even = side[0] == 0, side[1] == 0

    def own(f, carry):
        for k, (src, dst, off) in enumerate(((past, xp, 2), (future, xf, 0))):
            a, b = rows_odd[k, f, 0], rows_even[k, f, 0]
            put_taps(dst, f + off, 0, jnp.where(row_even, a, b))
            for r in range(rows):
                put_taps(dst, f + off, r + 1, src[f, r])
            put_taps(dst, f + off, rows + 1, jnp.where(row_even, b, a))
        return carry

    lax.fori_loop(0, frames, own, 0)

    def edge(f, carry):
        for dst, off, odd_first in ((xp, 0, True), (xf, frames, False)):
            pick = frame_even if odd_first else jnp.logical_not(frame_even)
            for r in range(rows):
                put_taps(dst, f + off, r + 1, jnp.where(pick, main_odd[f, r], main_even[f, r]))
            for s in range(2):
                put_taps(dst, f + off, s * (rows + 1), jnp.where(pick, rim_odd[f, s], rim_even[f, s]))
        return carry

    lax.fori_loop(0, 2, edge, 0)


def convolve(wp, wf, xp, xf, accp, accf):
    frames, rows = xp.shape[0] - 2, xp.shape[1] - 2
    taps, cols = 3 * xp.shape[2], xp.shape[3]
    chan = wp.shape[0] // 3
    accp[...] = jnp.zeros_like(accp)
    accf[...] = jnp.zeros_like(accf)

    def step(g, carry):
        for w, x, acc in ((wp, xp, accp), (wf, xf, accf)):
            for r in range(rows):
                part = jnp.dot(w[...], x[g, r : r + 3].reshape(taps, cols), preferred_element_type=F32)
                for t in range(3):
                    acc[g - t + 2, :, r * cols : (r + 1) * cols] += part[t * chan : (t + 1) * chan]
        return carry

    lax.fori_loop(0, frames + 2, step, 0)


def first_kernel(side, past, future, rows_odd, rows_even, main_odd, main_even, rim_odd, rim_even, wp, wf, bias,
                 active_out, pre_out, grads, xp, xf, accp, accf, upa, upg, d1, d2):
    frames, rows, chan, cols = past.shape
    build(side, past, future, rows_odd, rows_even, main_odd, main_even, rim_odd, rim_even, xp, xf)
    convolve(wp, wf, xp, xf, accp, accf)
    for up in (upa, upg):
        for f in (0, 1, frames + 2, frames + 3):
            up[f] = jnp.zeros(up.shape[1:], up.dtype)

    def point(f, total):
        for r in range(rows):
            span = slice(r * cols, (r + 1) * cols)
            hidden = accp[f + 2, :, span] + bias[...]
            sig = jax.nn.sigmoid(hidden)
            active = (hidden * sig).astype(BF16)
            pre = (accf[f + 2, :, span] * sig * (1.0 + hidden * (1.0 - sig))).astype(BF16)
            active_out[f, r] = active
            pre_out[f, r] = pre
            upa[f + 2, :, span] = active
            upg[f + 2, :, span] = pre
            total = total + pre.astype(F32)
        return total

    total = lax.fori_loop(0, frames, point, jnp.zeros((chan, cols), F32))
    bias_sum = jnp.sum(total, axis=1, keepdims=True)
    d1[...] = jnp.zeros_like(d1)
    d2[...] = jnp.zeros_like(d2)
    nt = (((1,), (1,)), ((), ()))

    def weigh(g, carry):
        pre3 = upg[pl.ds(g, 3)].reshape(3 * chan, rows * cols)
        act3 = upa[pl.ds(g, 3)].reshape(3 * chan, rows * cols)
        xc = jnp.concatenate([xp[g, r : r + 3].reshape(9 * chan, cols) for r in range(rows)], axis=1)
        d1[...] += lax.dot_general(pre3, xc, nt, preferred_element_type=F32)
        xo = jnp.concatenate([xf[g, r : r + 3].reshape(9 * chan, cols) for r in range(rows)], axis=1)
        d2[...] += lax.dot_general(xo, act3, nt, preferred_element_type=F32)
        return carry

    lax.fori_loop(0, frames + 2, weigh, 0)
    per = chan // grads.shape[1]
    for t in range(3):
        for ij in range(9):
            one = d1[(2 - t) * chan : (3 - t) * chan, ij * chan : (ij + 1) * chan]
            two = d2[(8 - ij) * chan : (9 - ij) * chan, t * chan : (t + 1) * chan]
            tap = (t * 9 + ij) * per
            both = jnp.concatenate([one, two], axis=1).astype(grads.dtype)
            grads[tap : tap + per] = both.reshape((per,) + grads.shape[1:])
    used = 27 * per
    grads[used : used + per] = jnp.broadcast_to(bias_sum, (chan, grads.shape[2])).astype(grads.dtype).reshape((per,) + grads.shape[1:])
    if used + per < grads.shape[0]:
        grads[used + per :] = jnp.zeros((grads.shape[0] - used - per,) + grads.shape[1:], grads.dtype)


def second_kernel(side, past, future, rows_odd, rows_even, main_odd, main_even, rim_odd, rim_even, wp, wf,
                  add_past, add_future, out_past, out_future, xp, xf, accp, accf):
    frames, rows, chan, cols = past.shape
    build(side, past, future, rows_odd, rows_even, main_odd, main_even, rim_odd, rim_even, xp, xf)
    convolve(wp, wf, xp, xf, accp, accf)

    def point(f, carry):
        for r in range(rows):
            span = slice(r * cols, (r + 1) * cols)
            out_past[f, r] = (add_past[f, r].astype(F32) + accp[f + 2, :, span]).astype(BF16)
            out_future[f, r] = (add_future[f, r].astype(F32) + accf[f + 2, :, span]).astype(BF16)
        return carry

    lax.fori_loop(0, frames, point, 0)


def specs(n):
    return [pl.BlockSpec(memory_space=pltpu.SMEM)] + [pl.BlockSpec(memory_space=pltpu.VMEM)] * (n - 1)


def shared_scratch(shape):
    frames, rows, chan, cols = shape
    return [pltpu.VMEM((frames + 2, rows + 2, 3 * chan, cols), BF16)] * 2 + [
        pltpu.VMEM((frames + 4, chan, rows * cols), F32)] * 2


def first_call(devices, *args):
    shape = args[1].shape
    frames, rows, chan, cols = shape
    return pl.pallas_call(
        first_kernel,
        out_shape=[jax.ShapeDtypeStruct(shape, BF16)] * 2 + [jax.ShapeDtypeStruct((devices, 16, 2 * chan), BF16)],
        in_specs=specs(len(args)), out_specs=[pl.BlockSpec(memory_space=pltpu.VMEM)] * 3,
        scratch_shapes=shared_scratch(shape) + [pltpu.VMEM((frames + 4, chan, rows * cols), BF16)] * 2
        + [pltpu.VMEM((3 * chan, 9 * chan), F32), pltpu.VMEM((9 * chan, 3 * chan), F32)],
        name="first",
    )(*args)


def second_call(*args):
    shape = args[1].shape
    return pl.pallas_call(
        second_kernel,
        out_shape=[jax.ShapeDtypeStruct(shape, BF16)] * 2,
        in_specs=specs(len(args)), out_specs=[pl.BlockSpec(memory_space=pltpu.VMEM)] * 2,
        scratch_shapes=shared_scratch(shape),
        name="second",
    )(*args)


def flat_forward(kernel):
    chan = kernel.shape[3]
    return jnp.transpose(kernel, (0, 3, 1, 2, 4)).reshape(3 * chan, 9 * chan)


def flat_adjoint(kernel):
    chan = kernel.shape[3]
    return jnp.transpose(kernel[::-1, ::-1, ::-1], (0, 4, 1, 2, 3)).reshape(3 * chan, 9 * chan)


AXES = ("frames", "rows")


def pairs_of(count, first):
    pairs = []
    for i in range(first, count - 1, 2):
        pairs += [(i, i + 1), (i + 1, i)]
    return pairs


def swap_neighbours(axis, even, to_next, to_prior):
    count = lax.axis_size(axis)
    with jax.named_scope("odd"):
        odd_pairs = lax.ppermute(jnp.where(even, to_prior, to_next), axis, pairs_of(count, 1))
    with jax.named_scope("even"):
        even_pairs = lax.ppermute(jnp.where(even, to_next, to_prior), axis, pairs_of(count, 0))
    return odd_pairs, even_pairs


def halo(side, past, future):
    row_even, frame_even = side[0] == 0, side[1] == 0
    both = jnp.stack([past, future])
    with jax.named_scope("rims_of_rows"):
        rows_odd, rows_even = swap_neighbours("rows", row_even, both[:, :, -1:], both[:, :, :1])
    with jax.named_scope("main"):
        main_odd, main_even = swap_neighbours("frames", frame_even, past[-2:], future[:2])
    low = jnp.where(row_even, rows_odd, rows_even)
    high = jnp.where(row_even, rows_even, rows_odd)
    rims = jnp.concatenate([low, high], axis=2)
    with jax.named_scope("rims_of_frames"):
        rim_odd, rim_even = swap_neighbours("frames", frame_even, rims[0, -2:], rims[1, :2])
    return rows_odd, rows_even, main_odd, main_even, rim_odd, rim_even


def total_over_devices(parts):
    with jax.named_scope("gather_terms"):
        mine = lax.all_to_all(parts, AXES, 0, 0, tiled=True)
    mine = jnp.sum(mine.astype(jnp.float32), axis=0).astype(jnp.bfloat16)
    spread = jnp.broadcast_to(mine[None], parts.shape)
    with jax.named_scope("spread_sums"):
        return lax.all_to_all(spread, AXES, 0, 0, tiled=True)


def per_device(clip_in, kernel_one, bias_one, kernel_two, cotangent):
    frame_count, row_count, channels, col_count = clip_in.shape
    devices = lax.axis_size("frames") * lax.axis_size("rows")
    side = jnp.stack([lax.axis_index("rows") % 2, lax.axis_index("frames") % 2]).astype(jnp.int32)
    with jax.named_scope("halo_one"):
        edges = halo(side, clip_in, cotangent)
    active, grad_pre, terms = first_call(
        devices, side, clip_in, cotangent, *edges,
        flat_forward(kernel_one), flat_adjoint(kernel_two), bias_one[:, None],
    )
    total = total_over_devices(terms)
    with jax.named_scope("halo_two"):
        edges = halo(side, active, grad_pre)
    block_out, grad_input = second_call(
        side, active, grad_pre, *edges,
        flat_forward(kernel_two), flat_adjoint(kernel_one), clip_in, cotangent,
    )
    cell_total = (
        frame_count * lax.axis_size("frames") * row_count * lax.axis_size("rows") * col_count
    )
    total = total.reshape((-1, 2 * channels)).astype(jnp.float32) * (1.0 / math.sqrt(cell_total))
    count = 27 * channels
    return (
        block_out,
        grad_input,
        total[:count, :channels].reshape(kernel_one.shape),
        total[:count, channels:].reshape(kernel_two.shape),
        total[count : count + channels, 0],
    )


def solution(mesh):
    in_specs = (P("frames", "rows", None, None), P(), P(), P(), P("frames", "rows", None, None))
    out_specs = (P("frames", "rows", None, None), P("frames", "rows", None, None), P(), P(), P())
    return jax.shard_map(
        per_device, mesh=mesh, in_specs=in_specs, out_specs=out_specs, check_vma=False
    )
```

```python
import math

import jax
import jax.numpy as jnp
from jax import lax
from jax.experimental import pallas as pl
from jax.experimental.pallas import tpu as pltpu
from jax.sharding import PartitionSpec as P

F32, BF16 = jnp.float32, jnp.bfloat16
NT = (((1,), (1,)), ((), ()))


def shifted(value, by):
    cols = value.shape[1]
    lane = lax.broadcasted_iota(jnp.int32, value.shape, 1)
    outside = lane == (0 if by == 1 else cols - 1)
    return jnp.where(outside, jnp.zeros_like(value), pltpu.roll(value, by % cols, 1))


def convolved(w, taps):
    part = jnp.dot(w[...], taps, preferred_element_type=F32)
    chan = w.shape[0] // 3
    return shifted(part[:chan], 1) + part[chan : 2 * chan] + shifted(part[2 * chan :], -1)


def column_taps(value):
    return jnp.concatenate([shifted(value, -1), value, shifted(value, 1)], axis=0)


def window(x, f, r):
    return x[f : f + 3, r : r + 3].reshape((-1, x.shape[3]))


def rim_window(x, f, r, rims, edge):
    rows = x.shape[1] - 2
    pieces = []
    for g in range(f, f + 3):
        if g not in edge:
            pieces.append(x[g, r : r + 3].reshape((-1, x.shape[3])))
            continue
        corner = rims(g - edge[0], 0 if r == 0 else 1)
        inner = x[g, 1:3] if r == 0 else x[g, rows - 1 : rows + 1]
        inner = inner.reshape((-1, x.shape[3]))
        pieces += [corner, inner] if r == 0 else [inner, corner]
    return jnp.concatenate(pieces, axis=0)


def extend(side, past, future, rows_odd, rows_even, main_odd, main_even, xp, xf):
    frames, rows = past.shape[0], past.shape[1]
    row_even, frame_even = side[0] == 0, side[1] == 0
    for f in range(frames):
        for k, (src, dst, off) in enumerate(((past, xp, 2), (future, xf, 0))):
            odd, even = rows_odd[k, f, 0], rows_even[k, f, 0]
            dst[f + off, 0] = jnp.where(row_even, odd, even)
            dst[f + off, 1 : rows + 1] = src[f]
            dst[f + off, rows + 1] = jnp.where(row_even, even, odd)
    for f in range(2):
        for r in range(rows):
            dst = jnp.where(frame_even, main_odd[f, r], main_even[f, r])
            xp[f, r + 1] = dst
            xf[f + frames, r + 1] = jnp.where(frame_even, main_even[f, r], main_odd[f, r])


def corner_rims(side, rim_odd, rim_even):
    even = side[1] == 0
    past = lambda f, s: jnp.where(even, rim_odd[f, s], rim_even[f, s])
    future = lambda f, s: jnp.where(even, rim_even[f, s], rim_odd[f, s])
    return past, future


def gated(hidden, grad_act):
    sig = jax.nn.sigmoid(hidden)
    return (hidden * sig).astype(BF16), (grad_act * sig * (1.0 + hidden * (1.0 - sig))).astype(BF16)


def weights_kernel(one, two, bias, one_fwd, one_adj, two_fwd, two_adj, bias_out):
    chan = one.shape[1]
    for src, fwd, adj in ((one, one_fwd, one_adj), (two, two_fwd, two_adj)):
        for t in range(3):
            for i in range(3):
                for j in range(3):
                    tap = src[t * 9 + i * 3 + j]
                    left = (t * 3 + i) * chan
                    fwd[j * chan : (j + 1) * chan, left : left + chan] = tap
                    left = (8 - t * 3 - i) * chan
                    flipped = jnp.transpose(tap.astype(F32)).astype(BF16)
                    adj[(2 - j) * chan : (3 - j) * chan, left : left + chan] = flipped
    spread = jnp.broadcast_to(bias[...], (chan, chan))
    lanes = lax.broadcasted_iota(jnp.int32, spread.shape, 1)
    keep = lanes == lax.broadcasted_iota(jnp.int32, spread.shape, 0)
    bias_out[...] = jnp.sum(jnp.where(keep, spread, 0.0), axis=1, keepdims=True)


def first_inner_kernel(side, past, future, rows_odd, rows_even, main_odd, main_even, wp, wf, bias,
                       active_out, pre_out, xp, xf, hid, act, d1, d2, bsum):
    frames, rows, chan, cols = past.shape
    extend(side, past, future, rows_odd, rows_even, main_odd, main_even, xp, xf)
    total = jnp.zeros((chan, cols), F32)
    pres, acts, winp, winf = [], [], [], []
    for f in range(frames):
        for r in range(1, rows - 1):
            winp.append(window(xp, f, r))
            winf.append(window(xf, f, r))
            active, pre = gated(convolved(wp, winp[-1]) + bias[...], convolved(wf, winf[-1]))
            active_out[f, r] = active
            pre_out[f, r] = pre
            acts.append(column_taps(active))
            pres.append(column_taps(pre))
            total = total + pre.astype(F32)
    for k in range(2):
        for s, r in enumerate((0, rows - 1)):
            hid[k, s] = convolved(wp, window(xp, frames - 2 + k, r)) + bias[...]
            act[k, s] = convolved(wf, window(xf, k, r))
    bsum[...] = total
    lanes = lambda parts: jnp.concatenate(parts, axis=1)
    d1[...] = lax.dot_general(lanes(pres), lanes(winp), NT, preferred_element_type=F32)
    d2[...] = lax.dot_general(lanes(winf), lanes(acts), NT, preferred_element_type=F32)


def first_outer_kernel(side, rim_odd, rim_even, xp, xf, hid, act, d1_in, d2_in, bsum, wp, wf, bias, active_in, pre_in,
                       active_out, pre_out, grads, d1, d2):
    frames, rows, chan, cols = active_out.shape
    past_rims, future_rims = corner_rims(side, rim_odd, rim_even)
    total = bsum[...]
    pres, acts, winp, winf = [], [], [], []
    for f in range(frames):
        for s, r in enumerate((0, rows - 1)):
            if f < 2:
                winp.append(rim_window(xp, f, r, past_rims, (0, 1)))
                hidden = convolved(wp, winp[-1]) + bias[...]
                winf.append(window(xf, f, r))
                grad_act = act[f, s]
            else:
                winp.append(window(xp, f, r))
                hidden = hid[f - frames + 2, s]
                winf.append(rim_window(xf, f, r, future_rims, (frames, frames + 1)))
                grad_act = convolved(wf, winf[-1])
            active, pre = gated(hidden, grad_act)
            active_out[f, r] = active
            pre_out[f, r] = pre
            acts.append(column_taps(active))
            pres.append(column_taps(pre))
            total = total + pre.astype(F32)
    for f in range(frames):
        for r in range(1, rows - 1):
            active_out[f, r] = active_in[f, r]
            pre_out[f, r] = pre_in[f, r]
    bias_sum = jnp.sum(total, axis=1, keepdims=True)
    lanes = lambda parts: jnp.concatenate(parts, axis=1)
    d1[...] = d1_in[...] + lax.dot_general(lanes(pres), lanes(winp), NT, preferred_element_type=F32)
    d2[...] = d2_in[...] + lax.dot_general(lanes(winf), lanes(acts), NT, preferred_element_type=F32)
    per = chan // grads.shape[1]
    for t in range(3):
        for i in range(3):
            for j in range(3):
                left, top = (t * 3 + i) * chan, (8 - t * 3 - i) * chan
                one = d1[j * chan : (j + 1) * chan, left : left + chan]
                two = d2[top : top + chan, (2 - j) * chan : (3 - j) * chan]
                tap = (t * 9 + i * 3 + j) * per
                both = jnp.concatenate([one, two], axis=1).astype(grads.dtype)
                grads[tap : tap + per] = both.reshape((per,) + grads.shape[1:])
    used = 27 * per
    bias_rows = jnp.broadcast_to(bias_sum, (chan, grads.shape[2])).astype(grads.dtype)
    grads[used : used + per] = bias_rows.reshape((per,) + grads.shape[1:])
    rest = grads.shape[0] - used - per
    if rest:
        grads[used + per :] = jnp.zeros((rest,) + grads.shape[1:], grads.dtype)


def second_inner_kernel(side, past, future, rows_odd, rows_even, main_odd, main_even, wp, wf, add_past, add_future,
                        out_past, out_future, xp, xf):
    frames, rows, chan, cols = past.shape
    extend(side, past, future, rows_odd, rows_even, main_odd, main_even, xp, xf)
    for f in range(frames):
        for r in range(rows):
            inner = 0 < r < rows - 1
            if f >= 2 or inner:
                out_past[f, r] = (add_past[f, r].astype(F32) + convolved(wp, window(xp, f, r))).astype(BF16)
            if f < frames - 2 or inner:
                out_future[f, r] = (add_future[f, r].astype(F32) + convolved(wf, window(xf, f, r))).astype(BF16)


def second_outer_kernel(side, rim_odd, rim_even, xp, xf, wp, wf, add_past, add_future, past_in, future_in,
                        out_past, out_future):
    frames, rows, chan, cols = out_past.shape
    past_rims, future_rims = corner_rims(side, rim_odd, rim_even)
    for f in range(2):
        for r in (0, rows - 1):
            taps = rim_window(xp, f, r, past_rims, (0, 1))
            out_past[f, r] = (add_past[f, r].astype(F32) + convolved(wp, taps)).astype(BF16)
            g = frames - 2 + f
            taps = rim_window(xf, g, r, future_rims, (frames, frames + 1))
            out_future[g, r] = (add_future[g, r].astype(F32) + convolved(wf, taps)).astype(BF16)
    for f in range(frames):
        for r in range(rows):
            inner = 0 < r < rows - 1
            if f >= 2 or inner:
                out_past[f, r] = past_in[f, r]
            if f < frames - 2 or inner:
                out_future[f, r] = future_in[f, r]


def call(kernel, outs, args, flops, scratch=(), scalars=1):
    vmem = pl.BlockSpec(memory_space=pltpu.VMEM)
    smem = pl.BlockSpec(memory_space=pltpu.SMEM)
    moved = sum(x.size * x.dtype.itemsize for x in list(args) + list(outs))
    return pl.pallas_call(
        kernel,
        out_shape=outs,
        in_specs=[smem] * scalars + [vmem] * (len(args) - scalars),
        out_specs=[vmem] * len(outs),
        scratch_shapes=scratch,
        compiler_params=pltpu.CompilerParams(vmem_limit_bytes=VMEM_LIMIT),
        cost_estimate=pl.CostEstimate(flops=flops, bytes_accessed=moved, transcendentals=0),
        name=kernel.__name__,
    )(*args)


VMEM_LIMIT = 24 * 1024 * 1024


def arrays(*shapes, kind=BF16):
    return [jax.ShapeDtypeStruct(shape, kind) for shape in shapes]


def flat_weights(one, two, bias):
    chan = bias.shape[0]
    taps = (27, chan, chan)
    outs = arrays(*[(3 * chan, 9 * chan)] * 4) + arrays((chan, 1), kind=F32)
    return call(weights_kernel, outs, (one.reshape(taps), two.reshape(taps), bias[None]), 0, scalars=0)


def conv_flops(shape, rows):
    return 2 * 27 * shape[2] * shape[2] * shape[3] * rows


def first_inner(side, past, future, edges, wp, wf, bias):
    shape = past.shape
    frames, rows, chan, cols = shape
    extended = (frames + 2, rows + 2, chan, cols)
    outs = arrays(shape, shape, extended, extended) + arrays(
        (2, 2, chan, cols), (2, 2, chan, cols), (3 * chan, 9 * chan), (9 * chan, 3 * chan), (chan, cols), kind=F32)
    return call(first_inner_kernel, outs, (side, past, future, *edges, wp, wf, bias), conv_flops(shape, 40))


def first_outer(devices, side, rims, inner, wp, wf, bias):
    active, pre, *rest = inner
    frames, rows, chan, cols = active.shape
    outs = arrays(active.shape, pre.shape, (devices, 16, 2 * chan))
    scratch = [pltpu.VMEM((3 * chan, 9 * chan), F32), pltpu.VMEM((9 * chan, 3 * chan), F32)]
    args = (side, *rims, *rest, wp, wf, bias, active, pre)
    return call(first_outer_kernel, outs, args, conv_flops(active.shape, 24), scratch)


def second_inner(side, past, future, edges, wp, wf, add_past, add_future):
    shape = past.shape
    frames, rows, chan, cols = shape
    extended = (frames + 2, rows + 2, chan, cols)
    args = (side, past, future, *edges, wp, wf, add_past, add_future)
    return call(second_inner_kernel, arrays(shape, shape, extended, extended), args, conv_flops(shape, 24))


def second_outer(side, rims, inner, wp, wf, add_past, add_future):
    out_past, out_future, xp, xf = inner
    args = (side, *rims, xp, xf, wp, wf, add_past, add_future, out_past, out_future)
    return call(second_outer_kernel, arrays(out_past.shape, out_past.shape), args, conv_flops(out_past.shape, 8))


AXES = ("frames", "rows")


def pairs_of(count, first):
    pairs = []
    for i in range(first, count - 1, 2):
        pairs += [(i, i + 1), (i + 1, i)]
    return pairs


def swap_neighbours(axis, even, to_next, to_prior):
    count = lax.axis_size(axis)
    with jax.named_scope("odd"):
        odd_pairs = lax.ppermute(jnp.where(even, to_prior, to_next), axis, pairs_of(count, 1))
    with jax.named_scope("even"):
        even_pairs = lax.ppermute(jnp.where(even, to_next, to_prior), axis, pairs_of(count, 0))
    return odd_pairs, even_pairs


def edges_of(side, past, future):
    both = jnp.stack([past, future])
    with jax.named_scope("rims_of_rows"):
        rows = swap_neighbours("rows", side[0] == 0, both[:, :, -1:], both[:, :, :1])
    with jax.named_scope("main"):
        main = swap_neighbours("frames", side[1] == 0, past[-2:], future[:2])
    return (*rows, *main)


def rims_of(side, rows_odd, rows_even):
    row_even = side[0] == 0
    low = jnp.where(row_even, rows_odd, rows_even)
    high = jnp.where(row_even, rows_even, rows_odd)
    rims = jnp.concatenate([low, high], axis=2)
    with jax.named_scope("rims_of_frames"):
        return swap_neighbours("frames", side[1] == 0, rims[0, -2:], rims[1, :2])


def total_over_devices(parts):
    with jax.named_scope("gather_terms"):
        mine = lax.all_to_all(parts, AXES, 0, 0, tiled=True)
    mine = jnp.sum(mine.astype(jnp.float32), axis=0).astype(jnp.bfloat16)
    spread = jnp.broadcast_to(mine[None], parts.shape)
    with jax.named_scope("spread_sums"):
        return lax.all_to_all(spread, AXES, 0, 0, tiled=True)


def per_device(clip_in, kernel_one, bias_one, kernel_two, cotangent):
    frame_count, row_count, channels, col_count = clip_in.shape
    devices = lax.axis_size("frames") * lax.axis_size("rows")
    side = jnp.stack([lax.axis_index("rows") % 2, lax.axis_index("frames") % 2]).astype(jnp.int32)
    with jax.named_scope("halo_one"):
        edges = edges_of(side, clip_in, cotangent)
    one_fwd, one_adj, two_fwd, two_adj, bias = flat_weights(kernel_one, kernel_two, bias_one)
    with jax.named_scope("halo_one"):
        rims = rims_of(side, *edges[:2])
    inner = first_inner(side, clip_in, cotangent, edges, one_fwd, two_adj, bias)
    active, grad_pre, terms = first_outer(devices, side, rims, inner, one_fwd, two_adj, bias)
    total = total_over_devices(terms)
    with jax.named_scope("halo_two"):
        edges = edges_of(side, active, grad_pre)
        rims = rims_of(side, *edges[:2])
    inner = second_inner(side, active, grad_pre, edges, two_fwd, one_adj, clip_in, cotangent)
    block_out, grad_input = second_outer(side, rims, inner, two_fwd, one_adj, clip_in, cotangent)
    cell_total = (
        frame_count * lax.axis_size("frames") * row_count * lax.axis_size("rows") * col_count
    )
    total = total.reshape((-1, 2 * channels)).astype(jnp.float32) * (1.0 / math.sqrt(cell_total))
    count = 27 * channels
    return (
        block_out,
        grad_input,
        total[:count, :channels].reshape(kernel_one.shape),
        total[:count, channels:].reshape(kernel_two.shape),
        total[count : count + channels, 0],
    )


def solution(mesh):
    in_specs = (P("frames", "rows", None, None), P(), P(), P(), P("frames", "rows", None, None))
    out_specs = (P("frames", "rows", None, None), P("frames", "rows", None, None), P(), P(), P())
    return jax.shard_map(
        per_device, mesh=mesh, in_specs=in_specs, out_specs=out_specs, check_vma=False
    )
```

```python
import functools
import math

import jax
import jax.numpy as jnp
from jax import lax
from jax.experimental import pallas as pl
from jax.experimental.pallas import tpu as pltpu
from jax.sharding import PartitionSpec as P

F32, BF16 = jnp.float32, jnp.bfloat16
NT = (((1,), (1,)), ((), ()))


def shifted(value, by):
    cols = value.shape[1]
    lane = lax.broadcasted_iota(jnp.int32, value.shape, 1)
    outside = lane == (0 if by == 1 else cols - 1)
    return jnp.where(outside, jnp.zeros_like(value), pltpu.roll(value, by % cols, 1))


def convolved(w, taps):
    part = jnp.dot(w[...], taps, preferred_element_type=F32)
    chan = w.shape[0] // 3
    return shifted(part[:chan], 1) + part[chan : 2 * chan] + shifted(part[2 * chan :], -1)


def column_taps(value):
    return jnp.concatenate([shifted(value, -1), value, shifted(value, 1)], axis=0)


def window(x, f, r):
    return x[f : f + 3, r : r + 3].reshape((-1, x.shape[3]))


def rim_window(x, f, r, rims, edge):
    rows = x.shape[1] - 2
    pieces = []
    for g in range(f, f + 3):
        if g not in edge:
            pieces.append(x[g, r : r + 3].reshape((-1, x.shape[3])))
            continue
        corner = rims(g - edge[0], 0 if r == 0 else 1)
        inner = x[g, 1:3] if r == 0 else x[g, rows - 1 : rows + 1]
        inner = inner.reshape((-1, x.shape[3]))
        pieces += [corner, inner] if r == 0 else [inner, corner]
    return jnp.concatenate(pieces, axis=0)


def extend(side, past, future, rows_odd, rows_even, main_odd, main_even, xp, xf):
    frames, rows = past.shape[0], past.shape[1]
    row_even, frame_even = side[0] == 0, side[1] == 0
    for f in range(frames):
        for k, (src, dst, off) in enumerate(((past, xp, 2), (future, xf, 0))):
            odd, even = rows_odd[k, f], rows_even[k, f]
            dst[f + off, 0] = jnp.where(row_even, odd, even)
            dst[f + off, 1 : rows + 1] = src[f]
            dst[f + off, rows + 1] = jnp.where(row_even, even, odd)
    for f in range(2):
        for r in range(rows):
            dst = jnp.where(frame_even, main_odd[f, r], main_even[f, r])
            xp[f, r + 1] = dst
            xf[f + frames, r + 1] = jnp.where(frame_even, main_even[f, r], main_odd[f, r])


def corner_rims(side, rim_odd, rim_even):
    even = side[1] == 0
    past = lambda f, s: jnp.where(even, rim_odd[f, s], rim_even[f, s])
    future = lambda f, s: jnp.where(even, rim_even[f, s], rim_odd[f, s])
    return past, future


def gated(hidden, grad_act):
    sig = jax.nn.sigmoid(hidden)
    return (hidden * sig).astype(BF16), (grad_act * sig * (1.0 + hidden * (1.0 - sig))).astype(BF16)


def rows_kernel(side, past, future, odd, even, sems):
    rows = past.shape[1]
    over_odd = side[0] * (rows - 1)
    copies = []
    for k, src in enumerate((past, future)):
        for s, (dst, r) in enumerate(((odd, over_odd), (even, rows - 1 - over_odd))):
            copies.append(pltpu.make_async_copy(src.at[:, r], dst.at[k], sems.at[k, s]))
    for copy in copies:
        copy.start()
    for copy in copies:
        copy.wait()


def rims_kernel(side, rows_odd, rows_even, odd, even):
    row_even, frame_even = side[0] == 0, side[1] == 0
    last = rows_odd.shape[1] - 2
    for f in range(2):
        for s in range(2):
            one, two = (rows_odd, rows_even) if s == 0 else (rows_even, rows_odd)
            past = jnp.where(row_even, one[0, f + last], two[0, f + last])
            future = jnp.where(row_even, one[1, f], two[1, f])
            odd[f, s] = jnp.where(frame_even, future, past)
            even[f, s] = jnp.where(frame_even, past, future)


def frames_kernel(side, past, future, rows_odd, rows_even, odd, even):
    row_even, frame_even = side[0] == 0, side[1] == 0
    frames, rows = past.shape[0], past.shape[1]
    for f in range(2):
        g = f + frames - 2
        for r in range(rows + 2):
            if 0 < r <= rows:
                one, two = past[g, r - 1], future[f, r - 1]
            else:
                a, b = (rows_odd, rows_even) if r == 0 else (rows_even, rows_odd)
                one = jnp.where(row_even, a[0, g], b[0, g])
                two = jnp.where(row_even, a[1, f], b[1, f])
            odd[f, r] = jnp.where(frame_even, two, one)
            even[f, r] = jnp.where(frame_even, one, two)


def weights_kernel(one, two, bias, one_fwd, one_adj, two_fwd, two_adj, bias_out):
    chan = one.shape[1]
    for src, fwd, adj in ((one, one_fwd, one_adj), (two, two_fwd, two_adj)):
        for t in range(3):
            for i in range(3):
                for j in range(3):
                    tap = src[t * 9 + i * 3 + j]
                    left = (t * 3 + i) * chan
                    fwd[j * chan : (j + 1) * chan, left : left + chan] = tap
                    left = (8 - t * 3 - i) * chan
                    flipped = jnp.transpose(tap.astype(F32)).astype(BF16)
                    adj[(2 - j) * chan : (3 - j) * chan, left : left + chan] = flipped
    spread = jnp.broadcast_to(bias[...], (chan, chan))
    lanes = lax.broadcasted_iota(jnp.int32, spread.shape, 1)
    keep = lanes == lax.broadcasted_iota(jnp.int32, spread.shape, 0)
    bias_out[...] = jnp.sum(jnp.where(keep, spread, 0.0), axis=1, keepdims=True)


def first_inner_kernel(side, past, future, rows_odd, rows_even, main_odd, main_even, wp, wf, bias,
                       active_out, pre_out, xp, xf, hid, act, d1, d2, bsum):
    frames, rows, chan, cols = past.shape
    extend(side, past, future, rows_odd, rows_even, main_odd, main_even, xp, xf)
    total = jnp.zeros((chan, cols), F32)
    pres, acts, winp, winf = [], [], [], []
    for f in range(frames):
        for r in range(1, rows - 1):
            winp.append(window(xp, f, r))
            winf.append(window(xf, f, r))
            active, pre = gated(convolved(wp, winp[-1]) + bias[...], convolved(wf, winf[-1]))
            active_out[f, r] = active
            pre_out[f, r] = pre
            acts.append(column_taps(active))
            pres.append(column_taps(pre))
            total = total + pre.astype(F32)
    for k in range(2):
        for s, r in enumerate((0, rows - 1)):
            hid[k, s] = convolved(wp, window(xp, frames - 2 + k, r)) + bias[...]
            act[k, s] = convolved(wf, window(xf, k, r))
    bsum[...] = total
    lanes = lambda parts: jnp.concatenate(parts, axis=1)
    d1[...] = lax.dot_general(lanes(pres), lanes(winp), NT, preferred_element_type=F32)
    d2[...] = lax.dot_general(lanes(winf), lanes(acts), NT, preferred_element_type=F32)


def first_outer_kernel(side, rim_odd, rim_even, xp, xf, hid, act, d1_in, d2_in, bsum, wp, wf, bias, active_in, pre_in,
                       active_out, pre_out, rows_odd, rows_even, grads, d1, d2):
    frames, rows, chan, cols = active_out.shape
    row_even = side[0] == 0
    past_rims, future_rims = corner_rims(side, rim_odd, rim_even)
    total = bsum[...]
    pres, acts, winp, winf = [], [], [], []
    for f in range(frames):
        ends_active, ends_pre = [], []
        for s, r in enumerate((0, rows - 1)):
            if f < 2:
                winp.append(rim_window(xp, f, r, past_rims, (0, 1)))
                hidden = convolved(wp, winp[-1]) + bias[...]
                winf.append(window(xf, f, r))
                grad_act = act[f, s]
            else:
                winp.append(window(xp, f, r))
                hidden = hid[f - frames + 2, s]
                winf.append(rim_window(xf, f, r, future_rims, (frames, frames + 1)))
                grad_act = convolved(wf, winf[-1])
            active, pre = gated(hidden, grad_act)
            active_out[f, r] = active
            pre_out[f, r] = pre
            ends_active.append(active)
            ends_pre.append(pre)
            acts.append(column_taps(active))
            pres.append(column_taps(pre))
            total = total + pre.astype(F32)
        for k, ends in enumerate((ends_active, ends_pre)):
            rows_odd[k, f] = jnp.where(row_even, ends[0], ends[1])
            rows_even[k, f] = jnp.where(row_even, ends[1], ends[0])
        for r in range(1, rows - 1):
            active_out[f, r] = active_in[f, r]
            pre_out[f, r] = pre_in[f, r]
    bias_sum = jnp.sum(total, axis=1, keepdims=True)
    lanes = lambda parts: jnp.concatenate(parts, axis=1)
    d1[...] = d1_in[...] + lax.dot_general(lanes(pres), lanes(winp), NT, preferred_element_type=F32)
    d2[...] = d2_in[...] + lax.dot_general(lanes(winf), lanes(acts), NT, preferred_element_type=F32)
    per = chan // grads.shape[1]
    for t in range(3):
        for i in range(3):
            for j in range(3):
                left, top = (t * 3 + i) * chan, (8 - t * 3 - i) * chan
                one = d1[j * chan : (j + 1) * chan, left : left + chan]
                two = d2[top : top + chan, (2 - j) * chan : (3 - j) * chan]
                tap = (t * 9 + i * 3 + j) * per
                both = jnp.concatenate([one, two], axis=1).astype(grads.dtype)
                grads[tap : tap + per] = both.reshape((per,) + grads.shape[1:])
    used = 27 * per
    bias_rows = jnp.broadcast_to(bias_sum, (chan, grads.shape[2])).astype(grads.dtype)
    grads[used : used + per] = bias_rows.reshape((per,) + grads.shape[1:])
    rest = grads.shape[0] - used - per
    if rest:
        grads[used + per :] = jnp.zeros((rest,) + grads.shape[1:], grads.dtype)


def extend_rows(side, past, future, rows_odd, rows_even, xp, xf):
    frames, rows = past.shape[0], past.shape[1]
    row_even = side[0] == 0
    for f in range(frames):
        for k, (src, dst) in enumerate(((past, xp), (future, xf))):
            odd, even = rows_odd[k, f], rows_even[k, f]
            dst[f, 0] = jnp.where(row_even, odd, even)
            dst[f, 1 : rows + 1] = src[f]
            dst[f, rows + 1] = jnp.where(row_even, even, odd)


def second_inner_kernel(side, past, future, rows_odd, rows_even, wp, wf, add_past, add_future,
                        out_past, out_future, xp, xf):
    frames, rows, chan, cols = past.shape
    extend_rows(side, past, future, rows_odd, rows_even, xp, xf)
    for f in range(frames - 2):
        for r in range(rows):
            g = f + 2
            out_past[g, r] = (add_past[g, r].astype(F32) + convolved(wp, window(xp, f, r))).astype(BF16)
            out_future[f, r] = (add_future[f, r].astype(F32) + convolved(wf, window(xf, f, r))).astype(BF16)


def second_outer_kernel(side, odd, even, xp, xf, wp, wf, add_past, add_future, past_in, future_in,
                        out_past, out_future, edge_past, edge_future):
    frames, rows, chan, cols = out_past.shape
    frame_even = side[1] == 0
    for f in range(2):
        for r in range(rows + 2):
            edge_past[f, r] = jnp.where(frame_even, odd[f, r], even[f, r])
            edge_future[f, r] = jnp.where(frame_even, even[f, r], odd[f, r])
    slab = lambda x, f, r: x[f, r : r + 3].reshape((3 * chan, cols))
    for f in range(2):
        for r in range(rows):
            pieces = [slab(edge_past, g, r) if g < 2 else slab(xp, g - 2, r) for g in range(f, f + 3)]
            taps = jnp.concatenate(pieces, axis=0)
            out_past[f, r] = (add_past[f, r].astype(F32) + convolved(wp, taps)).astype(BF16)
            k = frames - 2 + f
            pieces = [slab(xf, g, r) if g < frames else slab(edge_future, g - frames, r) for g in range(k, k + 3)]
            taps = jnp.concatenate(pieces, axis=0)
            out_future[k, r] = (add_future[k, r].astype(F32) + convolved(wf, taps)).astype(BF16)
    for f in range(frames - 2):
        out_past[f + 2] = past_in[f + 2]
        out_future[f] = future_in[f]


def sum_kernel(parts, out, *, scale):
    total = parts[0].astype(F32)
    for k in range(1, parts.shape[0]):
        total = total + parts[k].astype(F32)
    out[...] = jnp.broadcast_to((total * scale).astype(out.dtype)[None], out.shape)


def unpack_kernel(parts, one, two, bias):
    taps, chan = one.shape[0], one.shape[1]
    per = chan // parts.shape[1]
    for k in range(taps):
        both = parts[k * per : (k + 1) * per].astype(F32).reshape((chan, 2 * chan))
        one[k] = both[:, :chan]
        two[k] = both[:, chan:]
    column = parts[taps * per : (taps + 1) * per].astype(F32).reshape((chan, 2 * chan))[:, :chan]
    keep = lax.broadcasted_iota(jnp.int32, column.shape, 0) == lax.broadcasted_iota(jnp.int32, column.shape, 1)
    bias[...] = jnp.sum(jnp.where(keep, column, 0.0), axis=0, keepdims=True)


def sides():
    return lax.axis_index("rows") % 2, lax.axis_index("frames") % 2


def call(kernel, outs, args, flops, scratch=(), sided=True, whole=0, name=None):
    vmem = pl.BlockSpec(memory_space=pltpu.VMEM)
    moved = sum(x.size * x.dtype.itemsize for x in list(args) + list(outs))
    body = (lambda *refs: kernel(sides(), *refs)) if sided else kernel
    return pl.pallas_call(
        body,
        out_shape=outs,
        in_specs=[pl.BlockSpec(memory_space=pltpu.HBM)] * whole + [vmem] * (len(args) - whole),
        out_specs=[vmem] * len(outs),
        scratch_shapes=scratch,
        compiler_params=pltpu.CompilerParams(vmem_limit_bytes=None if whole else VMEM_LIMIT),
        cost_estimate=pl.CostEstimate(flops=flops, bytes_accessed=moved, transcendentals=0),
        name=name or kernel.__name__,
    )(*args)


VMEM_LIMIT = 24 * 1024 * 1024


def arrays(*shapes, kind=BF16):
    return [jax.ShapeDtypeStruct(shape, kind) for shape in shapes]


def flat_weights(one, two, bias):
    chan = bias.shape[0]
    taps = (27, chan, chan)
    outs = arrays(*[(3 * chan, 9 * chan)] * 4) + arrays((chan, 1), kind=F32)
    return call(weights_kernel, outs, (one.reshape(taps), two.reshape(taps), bias[None]), 0, sided=False)


def conv_flops(shape, rows):
    return 2 * 27 * shape[2] * shape[2] * shape[3] * rows


def first_inner(past, future, edges, wp, wf, bias):
    shape = past.shape
    frames, rows, chan, cols = shape
    extended = (frames + 2, rows + 2, chan, cols)
    outs = arrays(shape, shape, extended, extended) + arrays(
        (2, 2, chan, cols), (2, 2, chan, cols), (3 * chan, 9 * chan), (9 * chan, 3 * chan), (chan, cols), kind=F32)
    return call(first_inner_kernel, outs, (past, future, *edges, wp, wf, bias), conv_flops(shape, 40))


def first_outer(devices, rims, inner, wp, wf, bias):
    active, pre, *rest = inner
    frames, rows, chan, cols = active.shape
    ends = (2, frames, chan, cols)
    outs = arrays(active.shape, pre.shape, ends, ends, (devices, 16, 2 * chan))
    scratch = [pltpu.VMEM((3 * chan, 9 * chan), F32), pltpu.VMEM((9 * chan, 3 * chan), F32)]
    args = (*rims, *rest, wp, wf, bias, active, pre)
    return call(first_outer_kernel, outs, args, conv_flops(active.shape, 24), scratch)


def second_inner(past, future, edges, wp, wf, add_past, add_future):
    shape = past.shape
    frames, rows, chan, cols = shape
    extended = (frames, rows + 2, chan, cols)
    args = (past, future, *edges, wp, wf, add_past, add_future)
    return call(second_inner_kernel, arrays(shape, shape, extended, extended), args, conv_flops(shape, 16))


def second_outer(edges, inner, wp, wf, add_past, add_future):
    out_past, out_future, xp, xf = inner
    frames, rows, chan, cols = out_past.shape
    args = (*edges, xp, xf, wp, wf, add_past, add_future, out_past, out_future)
    scratch = [pltpu.VMEM((2, rows + 2, chan, cols), BF16)] * 2
    return call(second_outer_kernel, arrays(out_past.shape, out_past.shape), args, conv_flops(out_past.shape, 16), scratch)


def rows_to_send(past, future):
    frames, rows, chan, cols = past.shape
    ends = (2, frames, chan, cols)
    scratch = [pltpu.SemaphoreType.DMA((2, 2))]
    return call(rows_kernel, arrays(ends, ends), (past, future), 0, scratch, whole=2)


def rims_to_send(rows_odd, rows_even):
    rims = (2, 2) + rows_odd.shape[2:]
    return call(rims_kernel, arrays(rims, rims), (rows_odd, rows_even), 0)


def frames_to_send(past, future, rows_odd, rows_even):
    edge = (2, past.shape[1] + 2) + past.shape[2:]
    return call(frames_kernel, arrays(edge, edge), (past, future, rows_odd, rows_even), 0)


def summed(parts, scale):
    kernel = functools.partial(sum_kernel, scale=scale)
    return call(kernel, arrays(parts.shape), (parts,), 0, sided=False, name="sum_kernel")[0]


def unpacked(parts, chan):
    outs = arrays((27, chan, chan), (27, chan, chan), (1, chan), kind=F32)
    return call(unpack_kernel, outs, (parts,), 0, sided=False)


AXES = ("frames", "rows")


def pairs_of(count, first):
    pairs = []
    for i in range(first, count - 1, 2):
        pairs += [(i, i + 1), (i + 1, i)]
    return pairs


def swap(axis, odd, even):
    count = lax.axis_size(axis)
    with jax.named_scope("even"):
        even = lax.ppermute(even, axis, pairs_of(count, 0))
    with jax.named_scope("odd"):
        return lax.ppermute(odd, axis, pairs_of(count, 1)), even


def per_device(clip_in, kernel_one, bias_one, kernel_two, cotangent):
    frame_count, row_count, channels, col_count = clip_in.shape
    devices = lax.axis_size("frames") * lax.axis_size("rows")
    cell_total = (
        frame_count * lax.axis_size("frames") * row_count * lax.axis_size("rows") * col_count
    )
    frame_even = sides()[1] == 0
    with jax.named_scope("rows_one"):
        rows = swap("rows", *rows_to_send(clip_in, cotangent))
    past, future = clip_in[-2:], cotangent[:2]
    with jax.named_scope("frames_one"):
        main = swap("frames", jnp.where(frame_even, future, past), jnp.where(frame_even, past, future))
    with jax.named_scope("rims_one"):
        rims = swap("frames", *rims_to_send(*rows))
    one_fwd, one_adj, two_fwd, two_adj, bias = flat_weights(kernel_one, kernel_two, bias_one)
    inner = first_inner(clip_in, cotangent, (*rows, *main), one_fwd, two_adj, bias)
    active, grad_pre, *ends, terms = first_outer(devices, rims, inner, one_fwd, two_adj, bias)

    with jax.named_scope("gather_terms"):
        terms = lax.all_to_all(terms, AXES, 0, 0, tiled=True)
    spread = summed(terms, 1.0 / math.sqrt(cell_total))
    with jax.named_scope("spread_sums"):
        total = lax.all_to_all(spread, AXES, 0, 0, tiled=True)

    with jax.named_scope("rows_two"):
        rows = swap("rows", *ends)
    *rows, _ = lax.optimization_barrier((*rows, spread))
    with jax.named_scope("frames_two"):
        edges = swap("frames", *frames_to_send(active, grad_pre, *rows))
    inner = second_inner(active, grad_pre, rows, two_fwd, one_adj, clip_in, cotangent)
    block_out, grad_input = second_outer(edges, inner, two_fwd, one_adj, clip_in, cotangent)
    first, second, bias = unpacked(total, channels)
    return (
        block_out,
        grad_input,
        first.reshape(kernel_one.shape),
        second.reshape(kernel_two.shape),
        bias.reshape(bias_one.shape),
    )


def solution(mesh):
    in_specs = (P("frames", "rows", None, None), P(), P(), P(), P("frames", "rows", None, None))
    out_specs = (P("frames", "rows", None, None), P("frames", "rows", None, None), P(), P(), P())
    return jax.shard_map(
        per_device, mesh=mesh, in_specs=in_specs, out_specs=out_specs, check_vma=False
    )
```

```python
import functools
import math

import jax
import jax.numpy as jnp
from jax import lax
from jax.experimental import pallas as pl
from jax.experimental.pallas import tpu as pltpu
from jax.sharding import PartitionSpec as P

F32, BF16 = jnp.float32, jnp.bfloat16
NT = (((1,), (1,)), ((), ()))


def shifted(value, by):
    cols = value.shape[1]
    lane = lax.broadcasted_iota(jnp.int32, value.shape, 1)
    outside = lane == (0 if by == 1 else cols - 1)
    return jnp.where(outside, jnp.zeros_like(value), pltpu.roll(value, by % cols, 1))


def convolved(w, taps):
    part = jnp.dot(w[...], taps, preferred_element_type=F32)
    chan = w.shape[0] // 3
    return shifted(part[:chan], 1) + part[chan : 2 * chan] + shifted(part[2 * chan :], -1)


def column_taps(value):
    return jnp.concatenate([shifted(value, -1), value, shifted(value, 1)], axis=0)


def picker(even, odd_ref, even_ref, swapped):
    one, two = (even_ref, odd_ref) if swapped else (odd_ref, even_ref)
    return lambda *at: jnp.where(even, one[at], two[at])


def field(own, before, after, corner):
    frames, rows, _, cols = own.shape

    def rows_of(g, low, high):
        first = 0 if before is None else before.shape[0]
        if g < first:
            return before[g, low:high]
        if g < first + frames:
            return own[g - first, low:high]
        return after[g - first - frames, low:high]

    def taps(f, r):
        pieces = []
        for g in range(f, f + 3):
            if r == 0:
                pieces.append(corner(g, 0))
            pieces.append(rows_of(g, max(r - 1, 0), min(r + 2, rows)).reshape((-1, cols)))
            if r == rows - 1:
                pieces.append(corner(g, 1))
        return jnp.concatenate(pieces, axis=0)

    return taps


def corners(side, frames, rows_odd, rows_even, rim_odd=None, rim_even=None):
    low = picker(side[0] == 0, rows_odd, rows_even, False)
    high = picker(side[0] == 0, rows_odd, rows_even, True)
    past_rim = picker(side[1] == 0, rim_odd, rim_even, False)
    future_rim = picker(side[1] == 0, rim_odd, rim_even, True)
    past = lambda g, s: past_rim(g, s) if g < 2 else (low, high)[s](0, g - 2)
    future = lambda g, s: future_rim(g - frames, s) if g >= frames else (low, high)[s](1, g)
    return past, future


def pick_main(side, main_odd, main_even, before, after):
    even = side[1] == 0
    past = picker(even, main_odd, main_even, False)
    future = picker(even, main_odd, main_even, True)
    for f in range(before.shape[0]):
        for r in range(before.shape[1]):
            before[f, r] = past(f, r)
            after[f, r] = future(f, r)


def gated(hidden, grad_act):
    sig = jax.nn.sigmoid(hidden)
    return (hidden * sig).astype(BF16), (grad_act * sig * (1.0 + hidden * (1.0 - sig))).astype(BF16)


def pack_kernel(side, past, future, rows_odd, rows_even, main_odd, main_even, sems):
    frames, rows = past.shape[0], past.shape[1]
    over_odd = side[0] * (rows - 1)

    def run(first, second):
        copies = [
            pltpu.make_async_copy(first, main_odd, sems.at[4]),
            pltpu.make_async_copy(second, main_even, sems.at[5]),
        ]
        for k, src in enumerate((past, future)):
            copies.append(pltpu.make_async_copy(src.at[:, over_odd], rows_odd.at[k], sems.at[2 * k]))
            over_even = rows - 1 - over_odd
            copies.append(pltpu.make_async_copy(src.at[:, over_even], rows_even.at[k], sems.at[2 * k + 1]))
        for copy in copies:
            copy.start()
        for copy in copies:
            copy.wait()

    last, first = past.at[frames - 2 : frames], future.at[0:2]
    pl.when(side[1] == 0)(lambda: run(first, last))
    pl.when(side[1] != 0)(lambda: run(last, first))


def repack_kernel(side, past, future, rows_odd, rows_even, main_odd, main_even):
    frames, rows = past.shape[0], past.shape[1]
    row_even, frame_even = side[0] == 0, side[1] == 0
    for f in range(frames):
        for k, src in enumerate((past, future)):
            low, high = src[f, 0], src[f, rows - 1]
            rows_odd[k, f] = jnp.where(row_even, low, high)
            rows_even[k, f] = jnp.where(row_even, high, low)
    for f in range(2):
        for r in range(rows):
            last, first = past[f + frames - 2, r], future[f, r]
            main_odd[f, r] = jnp.where(frame_even, first, last)
            main_even[f, r] = jnp.where(frame_even, last, first)


def rims_kernel(side, rows_odd, rows_even, odd, even):
    row_even, frame_even = side[0] == 0, side[1] == 0
    last = rows_odd.shape[1] - 2
    for f in range(2):
        for s in range(2):
            one, two = (rows_odd, rows_even) if s == 0 else (rows_even, rows_odd)
            past = jnp.where(row_even, one[0, f + last], two[0, f + last])
            future = jnp.where(row_even, one[1, f], two[1, f])
            odd[f, s] = jnp.where(frame_even, future, past)
            even[f, s] = jnp.where(frame_even, past, future)


def weights_kernel(one, two, bias, one_fwd, one_adj, two_fwd, two_adj, bias_out):
    chan = one.shape[1]
    for src, fwd, adj in ((one, one_fwd, one_adj), (two, two_fwd, two_adj)):
        for t in range(3):
            for i in range(3):
                for j in range(3):
                    tap = src[t * 9 + i * 3 + j]
                    left = (t * 3 + i) * chan
                    fwd[j * chan : (j + 1) * chan, left : left + chan] = tap
                    left = (8 - t * 3 - i) * chan
                    flipped = jnp.transpose(tap.astype(F32)).astype(BF16)
                    adj[(2 - j) * chan : (3 - j) * chan, left : left + chan] = flipped
    spread = jnp.broadcast_to(bias[...], (chan, chan))
    lanes = lax.broadcasted_iota(jnp.int32, spread.shape, 1)
    keep = lanes == lax.broadcasted_iota(jnp.int32, spread.shape, 0)
    bias_out[...] = jnp.sum(jnp.where(keep, spread, 0.0), axis=1, keepdims=True)


def first_inner_kernel(side, past, future, main_odd, main_even, wp, wf, bias,
                       active_out, pre_out, before, after, d1, d2, bsum):
    frames, rows, chan, cols = past.shape
    pick_main(side, main_odd, main_even, before, after)
    past_taps = field(past, before, None, None)
    future_taps = field(future, None, after, None)
    total = jnp.zeros((chan, cols), F32)
    pres, acts, winp, winf = [], [], [], []
    for f in range(frames):
        for r in range(1, rows - 1):
            winp.append(past_taps(f, r))
            winf.append(future_taps(f, r))
            active, pre = gated(convolved(wp, winp[-1]) + bias[...], convolved(wf, winf[-1]))
            active_out[f, r] = active
            pre_out[f, r] = pre
            acts.append(column_taps(active))
            pres.append(column_taps(pre))
            total = total + pre.astype(F32)
    bsum[...] = total
    lanes = lambda parts: jnp.concatenate(parts, axis=1)
    d1[...] = lax.dot_general(lanes(pres), lanes(winp), NT, preferred_element_type=F32)
    d2[...] = lax.dot_general(lanes(winf), lanes(acts), NT, preferred_element_type=F32)


def first_middle_kernel(side, past, future, rows_odd, rows_even, wp, wf, bias, hid, act):
    frames, rows, _, _ = past.shape
    past_corner, future_corner = corners(side, frames, rows_odd, rows_even)
    past_taps = field(past, past.at[0:2], None, past_corner)
    future_taps = field(future, None, future, future_corner)
    for k in range(2):
        for s, r in enumerate((0, rows - 1)):
            hid[k, s] = convolved(wp, past_taps(frames - 2 + k, r)) + bias[...]
            act[k, s] = convolved(wf, future_taps(k, r))


def first_outer_kernel(side, rim_odd, rim_even, rows_in_odd, rows_in_even, past, future, before, after, hid, act,
                       d1_in, d2_in, bsum, wp, wf, bias, active_in, pre_in,
                       active_out, pre_out, grads, d1, d2):
    frames, rows, chan, _ = active_out.shape
    past_corner, future_corner = corners(side, frames, rows_in_odd, rows_in_even, rim_odd, rim_even)
    past_taps = field(past, before, None, past_corner)
    future_taps = field(future, None, after, future_corner)
    total = bsum[...]
    pres, acts, winp, winf = [], [], [], []
    for f in range(frames):
        for s, r in enumerate((0, rows - 1)):
            winp.append(past_taps(f, r))
            winf.append(future_taps(f, r))
            hidden = convolved(wp, winp[-1]) + bias[...] if f < 2 else hid[f - frames + 2, s]
            grad_act = act[f, s] if f < 2 else convolved(wf, winf[-1])
            active, pre = gated(hidden, grad_act)
            active_out[f, r] = active
            pre_out[f, r] = pre
            acts.append(column_taps(active))
            pres.append(column_taps(pre))
            total = total + pre.astype(F32)
        for r in range(1, rows - 1):
            active_out[f, r] = active_in[f, r]
            pre_out[f, r] = pre_in[f, r]
    bias_sum = jnp.sum(total, axis=1, keepdims=True)
    lanes = lambda parts: jnp.concatenate(parts, axis=1)
    d1[...] = d1_in[...] + lax.dot_general(lanes(pres), lanes(winp), NT, preferred_element_type=F32)
    d2[...] = d2_in[...] + lax.dot_general(lanes(winf), lanes(acts), NT, preferred_element_type=F32)
    per = chan // grads.shape[1]
    for t in range(3):
        for i in range(3):
            for j in range(3):
                left, top = (t * 3 + i) * chan, (8 - t * 3 - i) * chan
                one = d1[j * chan : (j + 1) * chan, left : left + chan]
                two = d2[top : top + chan, (2 - j) * chan : (3 - j) * chan]
                tap = (t * 9 + i * 3 + j) * per
                both = jnp.concatenate([one, two], axis=1).astype(grads.dtype)
                grads[tap : tap + per] = both.reshape((per,) + grads.shape[1:])
    used = 27 * per
    bias_rows = jnp.broadcast_to(bias_sum, (chan, grads.shape[2])).astype(grads.dtype)
    grads[used : used + per] = bias_rows.reshape((per,) + grads.shape[1:])
    rest = grads.shape[0] - used - per
    if rest:
        grads[used + per :] = jnp.zeros((rest,) + grads.shape[1:], grads.dtype)


def second_inner_kernel(side, past, future, rows_odd, rows_even, main_odd, main_even, wp, wf, add_past, add_future,
                        out_past, out_future, before, after):
    frames, rows, _, _ = past.shape
    pick_main(side, main_odd, main_even, before, after)
    past_corner, future_corner = corners(side, frames, rows_odd, rows_even)
    past_taps = field(past, before, None, past_corner)
    future_taps = field(future, None, after, future_corner)
    for f in range(frames):
        for r in range(rows):
            inner = 0 < r < rows - 1
            if f >= 2 or inner:
                out_past[f, r] = (add_past[f, r].astype(F32) + convolved(wp, past_taps(f, r))).astype(BF16)
            if f < frames - 2 or inner:
                out_future[f, r] = (add_future[f, r].astype(F32) + convolved(wf, future_taps(f, r))).astype(BF16)


def second_outer_kernel(side, rim_odd, rim_even, past, future, rows_odd, rows_even, before, after, wp, wf,
                        add_past, add_future, past_in, future_in, out_past, out_future):
    frames, rows, _, _ = out_past.shape
    past_corner, future_corner = corners(side, frames, rows_odd, rows_even, rim_odd, rim_even)
    past_taps = field(past, before, None, past_corner)
    future_taps = field(future, None, after, future_corner)
    for f in range(2):
        for r in (0, rows - 1):
            g = frames - 2 + f
            out_past[f, r] = (add_past[f, r].astype(F32) + convolved(wp, past_taps(f, r))).astype(BF16)
            out_future[g, r] = (add_future[g, r].astype(F32) + convolved(wf, future_taps(g, r))).astype(BF16)
    for f in range(frames):
        for r in range(rows):
            inner = 0 < r < rows - 1
            if f >= 2 or inner:
                out_past[f, r] = past_in[f, r]
            if f < frames - 2 or inner:
                out_future[f, r] = future_in[f, r]


def sum_kernel(parts, out, *, scale):
    total = parts[0].astype(F32)
    for k in range(1, parts.shape[0]):
        total = total + parts[k].astype(F32)
    out[...] = jnp.broadcast_to((total * scale).astype(out.dtype)[None], out.shape)


def unpack_kernel(parts, one, two, bias):
    taps, chan = one.shape[0], one.shape[1]
    per = chan // parts.shape[1]
    for k in range(taps):
        both = parts[k * per : (k + 1) * per].astype(F32).reshape((chan, 2 * chan))
        one[k] = both[:, :chan]
        two[k] = both[:, chan:]
    column = parts[taps * per : (taps + 1) * per].astype(F32).reshape((chan, 2 * chan))[:, :chan]
    keep = lax.broadcasted_iota(jnp.int32, column.shape, 0) == lax.broadcasted_iota(jnp.int32, column.shape, 1)
    bias[...] = jnp.sum(jnp.where(keep, column, 0.0), axis=0, keepdims=True)


def sides():
    return lax.axis_index("rows") % 2, lax.axis_index("frames") % 2


def call(kernel, outs, args, flops, scratch=(), sided=True, whole=0):
    vmem = pl.BlockSpec(memory_space=pltpu.VMEM)
    moved = sum(x.size * x.dtype.itemsize for x in list(args) + list(outs))
    body = (lambda *refs: kernel(sides(), *refs)) if sided else kernel
    return pl.pallas_call(
        body,
        out_shape=outs,
        in_specs=[pl.BlockSpec(memory_space=pltpu.HBM)] * whole + [vmem] * (len(args) - whole),
        out_specs=[vmem] * len(outs),
        scratch_shapes=scratch,
        compiler_params=pltpu.CompilerParams(vmem_limit_bytes=None if whole else VMEM_LIMIT),
        cost_estimate=pl.CostEstimate(flops=flops, bytes_accessed=moved, transcendentals=0),
    )(*args)


VMEM_LIMIT = 24 * 1024 * 1024


def arrays(*shapes, kind=BF16):
    return [jax.ShapeDtypeStruct(shape, kind) for shape in shapes]


def flat_weights(one, two, bias):
    chan = bias.shape[0]
    taps = (27, chan, chan)
    outs = arrays(*[(3 * chan, 9 * chan)] * 4) + arrays((chan, 1), kind=F32)
    return call(weights_kernel, outs, (one.reshape(taps), two.reshape(taps), bias[None]), 0, sided=False)


def conv_flops(shape, rows):
    return 2 * 27 * shape[2] * shape[2] * shape[3] * rows


def frame_pair(shape):
    return (2,) + shape[1:]


def first_inner(past, future, main, wp, wf, bias):
    shape = past.shape
    chan, cols = shape[2:]
    outs = arrays(shape, shape, frame_pair(shape), frame_pair(shape)) + arrays(
        (3 * chan, 9 * chan), (9 * chan, 3 * chan), (chan, cols), kind=F32)
    return call(first_inner_kernel, outs, (past, future, *main, wp, wf, bias), conv_flops(shape, 32))


def first_middle(past, future, rows, wp, wf, bias):
    part = (2, 2) + past.shape[2:]
    return call(first_middle_kernel, arrays(part, part, kind=F32), (past, future, *rows, wp, wf, bias),
                conv_flops(past.shape, 8))


def first_outer(devices, past, future, rows, rims, inner, middle, wp, wf, bias):
    active, pre, before, after, *sums = inner
    _, _, chan, _ = active.shape
    outs = arrays(active.shape, pre.shape, (devices, 16, 2 * chan))
    scratch = [pltpu.VMEM((3 * chan, 9 * chan), F32), pltpu.VMEM((9 * chan, 3 * chan), F32)]
    args = (*rims, *rows, past, future, before, after, *middle, *sums, wp, wf, bias, active, pre)
    return call(first_outer_kernel, outs, args, conv_flops(active.shape, 24), scratch)


def second_inner(past, future, rows, main, wp, wf, add_past, add_future):
    shape = past.shape
    outs = arrays(shape, shape, frame_pair(shape), frame_pair(shape))
    args = (past, future, *rows, *main, wp, wf, add_past, add_future)
    return call(second_inner_kernel, outs, args, conv_flops(shape, 24))


def second_outer(past, future, rows, rims, inner, wp, wf, add_past, add_future):
    out_past, out_future, before, after = inner
    args = (*rims, past, future, *rows, before, after, wp, wf, add_past, add_future, out_past, out_future)
    return call(second_outer_kernel, arrays(out_past.shape, out_past.shape), args, conv_flops(out_past.shape, 8))


def pack(past, future):
    frames, _, chan, cols = past.shape
    ends = (2, frames, chan, cols)
    scratch = [pltpu.SemaphoreType.DMA((6,))]
    outs = arrays(ends, ends, frame_pair(past.shape), frame_pair(past.shape))
    return call(pack_kernel, outs, (past, future), 0, scratch, whole=2)


def repack(past, future):
    frames, _, chan, cols = past.shape
    ends = (2, frames, chan, cols)
    outs = arrays(ends, ends, frame_pair(past.shape), frame_pair(past.shape))
    return call(repack_kernel, outs, (past, future), 0)


def rims_to_send(rows_odd, rows_even):
    rims = (2, 2) + rows_odd.shape[2:]
    return call(rims_kernel, arrays(rims, rims), (rows_odd, rows_even), 0)


def summed(parts, scale):
    kernel = functools.partial(sum_kernel, scale=scale)
    return call(kernel, arrays(parts.shape), (parts,), 0, sided=False)[0]


def unpacked(parts, chan):
    outs = arrays((27, chan, chan), (27, chan, chan), (1, chan), kind=F32)
    return call(unpack_kernel, outs, (parts,), 0, sided=False)


AXES = ("frames", "rows")


def pairs_of(count, first):
    pairs = []
    for i in range(first, count - 1, 2):
        pairs += [(i, i + 1), (i + 1, i)]
    return pairs


def swap(axis, odd, even):
    count = lax.axis_size(axis)
    even = lax.ppermute(even, axis, pairs_of(count, 0))
    return lax.ppermute(odd, axis, pairs_of(count, 1)), even


def per_device(clip_in, kernel_one, bias_one, kernel_two, cotangent):
    frame_count, row_count, channels, col_count = clip_in.shape
    devices = lax.axis_size("frames") * lax.axis_size("rows")
    cell_total = (
        frame_count * lax.axis_size("frames") * row_count * lax.axis_size("rows") * col_count
    )
    rows_odd, rows_even, main_odd, main_even = pack(clip_in, cotangent)
    main = swap("frames", main_odd, main_even)
    rows = swap("rows", rows_odd, rows_even)
    one_fwd, one_adj, two_fwd, two_adj, bias = flat_weights(kernel_one, kernel_two, bias_one)
    inner = first_inner(clip_in, cotangent, main, one_fwd, two_adj, bias)
    *rows, _ = lax.optimization_barrier((*rows, inner[-1]))
    rims = swap("frames", *rims_to_send(*rows))
    middle = first_middle(clip_in, cotangent, rows, one_fwd, two_adj, bias)
    active, grad_pre, terms = first_outer(
        devices, clip_in, cotangent, rows, rims, inner, middle, one_fwd, two_adj, bias
    )

    terms = lax.all_to_all(terms, AXES, 0, 0, tiled=True)
    spread = summed(terms, 1.0 / math.sqrt(cell_total))
    total = lax.all_to_all(spread, AXES, 0, 0, tiled=True)

    rows_odd, rows_even, main_odd, main_even = repack(active, grad_pre)
    rows = swap("rows", rows_odd, rows_even)
    main = swap("frames", main_odd, main_even)
    *rows, _ = lax.optimization_barrier((*rows, spread))
    rims = swap("frames", *rims_to_send(*rows))
    inner = second_inner(active, grad_pre, rows, main, two_fwd, one_adj, clip_in, cotangent)
    block_out, grad_input = second_outer(
        active, grad_pre, rows, rims, inner, two_fwd, one_adj, clip_in, cotangent
    )
    first, second, bias = unpacked(total, channels)
    return (
        block_out,
        grad_input,
        first.reshape(kernel_one.shape),
        second.reshape(kernel_two.shape),
        bias.reshape(bias_one.shape),
    )


def solution(mesh):
    in_specs = (P("frames", "rows", None, None), P(), P(), P(), P("frames", "rows", None, None))
    out_specs = (P("frames", "rows", None, None), P("frames", "rows", None, None), P(), P(), P())
    return jax.shard_map(per_device, mesh=mesh, in_specs=in_specs, out_specs=out_specs, check_vma=False)
```

```python
import functools
import math

import jax
import jax.numpy as jnp
from jax import lax
from jax.experimental import pallas as pl
from jax.experimental.pallas import tpu as pltpu
from jax.sharding import PartitionSpec as P

F32, BF16 = jnp.float32, jnp.bfloat16
NT = (((1,), (1,)), ((), ()))


def shifted(value, by):
    cols = value.shape[1]
    lane = lax.broadcasted_iota(jnp.int32, value.shape, 1)
    outside = lane == (0 if by == 1 else cols - 1)
    return jnp.where(outside, jnp.zeros_like(value), pltpu.roll(value, by % cols, 1))


def convolved(w, taps):
    part = jnp.dot(w[...], taps, preferred_element_type=F32)
    chan = w.shape[0] // 3
    return shifted(part[:chan], 1) + part[chan : 2 * chan] + shifted(part[2 * chan :], -1)


def column_taps(value):
    return jnp.concatenate([shifted(value, -1), value, shifted(value, 1)], axis=0)


def slab_of(ref, *at):
    return ref[at + (0,) * (len(ref.shape) - 2 - len(at))]


def picker(even, odd_ref, even_ref, swapped):
    one, two = (even_ref, odd_ref) if swapped else (odd_ref, even_ref)
    return lambda *at: jnp.where(even, slab_of(one, *at), slab_of(two, *at))


def field(own, before, after, corner):
    frames, rows, _, cols = own.shape

    def rows_of(g, low, high):
        first = 0 if before is None else before.shape[0]
        if g < first:
            return before[g, low:high]
        if g < first + frames:
            return own[g - first, low:high]
        return after[g - first - frames, low:high]

    def taps(f, r):
        pieces = []
        for g in range(f, f + 3):
            if r == 0:
                pieces.append(corner(g, 0))
            pieces.append(rows_of(g, max(r - 1, 0), min(r + 2, rows)).reshape((-1, cols)))
            if r == rows - 1:
                pieces.append(corner(g, 1))
        return jnp.concatenate(pieces, axis=0)

    return taps


def corners(side, frames, rows_odd, rows_even, rim_odd=None, rim_even=None):
    low = picker(side[0] == 0, rows_odd, rows_even, False)
    high = picker(side[0] == 0, rows_odd, rows_even, True)
    past_rim = picker(side[1] == 0, rim_odd, rim_even, False)
    future_rim = picker(side[1] == 0, rim_odd, rim_even, True)
    past = lambda g, s: past_rim(g, s) if g < 2 else (low, high)[s](0, g - 2)
    future = lambda g, s: future_rim(g - frames, s) if g >= frames else (low, high)[s](1, g)
    return past, future


def pick_main(side, main_odd, main_even, before, after):
    even = side[1] == 0
    past = picker(even, main_odd, main_even, False)
    future = picker(even, main_odd, main_even, True)
    for f in range(before.shape[0]):
        for r in range(before.shape[1]):
            before[f, r] = past(f, r)
            after[f, r] = future(f, r)


def gated(hidden, grad_act):
    sig = jax.nn.sigmoid(hidden)
    return (hidden * sig).astype(BF16), (grad_act * sig * (1.0 + hidden * (1.0 - sig))).astype(BF16)


def repack_kernel(side, past, future, rows_odd, rows_even, main_odd, main_even):
    frames, rows = past.shape[0], past.shape[1]
    row_even, frame_even = side[0] == 0, side[1] == 0
    for f in range(frames):
        for k, src in enumerate((past, future)):
            low, high = src[f, 0], src[f, rows - 1]
            rows_odd[k, f] = jnp.where(row_even, low, high)
            rows_even[k, f] = jnp.where(row_even, high, low)
    for f in range(2):
        for r in range(rows):
            last, first = past[f + frames - 2, r], future[f, r]
            main_odd[f, r] = jnp.where(frame_even, first, last)
            main_even[f, r] = jnp.where(frame_even, last, first)


def rims_kernel(side, rows_odd, rows_even, odd, even):
    frame_even = side[1] == 0
    last = rows_odd.shape[1] - 2
    low = picker(side[0] == 0, rows_odd, rows_even, False)
    high = picker(side[0] == 0, rows_odd, rows_even, True)
    for f in range(2):
        for s, rim in enumerate((low, high)):
            past, future = rim(0, f + last), rim(1, f)
            odd[f, s] = jnp.where(frame_even, future, past)
            even[f, s] = jnp.where(frame_even, past, future)


def weights_kernel(one, two, one_fwd, one_adj, two_fwd, two_adj):
    chan = one.shape[1]
    for src, fwd, adj in ((one, one_fwd, one_adj), (two, two_fwd, two_adj)):
        for t in range(3):
            for i in range(3):
                for j in range(3):
                    tap = src[t * 9 + i * 3 + j]
                    left = (t * 3 + i) * chan
                    fwd[j * chan : (j + 1) * chan, left : left + chan] = tap
                    left = (8 - t * 3 - i) * chan
                    flipped = jnp.transpose(tap.astype(F32)).astype(BF16)
                    adj[(2 - j) * chan : (3 - j) * chan, left : left + chan] = flipped


def column(row):
    n = row.shape[1]
    spread = jnp.broadcast_to(row, (n, n))
    keep = lax.broadcasted_iota(jnp.int32, (n, n), 0) == lax.broadcasted_iota(jnp.int32, (n, n), 1)
    return jnp.sum(jnp.where(keep, spread, 0.0), axis=1, keepdims=True)


def first_inner_kernel(side, past, future, main_odd, main_even, wp, wf, bias,
                       active_out, pre_out, before, after, d1, d2, bsum):
    frames, rows, chan, cols = past.shape
    pick_main(side, main_odd, main_even, before, after)
    past_taps = field(past, before, None, None)
    future_taps = field(future, None, after, None)
    shift = column(bias[...])
    total = jnp.zeros((chan, cols), F32)
    pres, acts, winp, winf = [], [], [], []
    for f in range(frames):
        for r in range(1, rows - 1):
            winp.append(past_taps(f, r))
            winf.append(future_taps(f, r))
            active, pre = gated(convolved(wp, winp[-1]) + shift, convolved(wf, winf[-1]))
            active_out[f, r] = active
            pre_out[f, r] = pre
            acts.append(column_taps(active))
            pres.append(column_taps(pre))
            total = total + pre.astype(F32)
    bsum[...] = total
    lanes = lambda parts: jnp.concatenate(parts, axis=1)
    d1[...] = lax.dot_general(lanes(pres), lanes(winp), NT, preferred_element_type=F32)
    d2[...] = lax.dot_general(lanes(winf), lanes(acts), NT, preferred_element_type=F32)


def first_middle_kernel(side, past, future, rows_odd, rows_even, wp, wf, bias, hid, act):
    frames, rows, _, _ = past.shape
    past_corner, future_corner = corners(side, frames, rows_odd, rows_even)
    past_taps = field(past, past.at[0:2], None, past_corner)
    future_taps = field(future, None, future, future_corner)
    shift = column(bias[...])
    for k in range(2):
        for s, r in enumerate((0, rows - 1)):
            hid[k, s] = convolved(wp, past_taps(frames - 2 + k, r)) + shift
            act[k, s] = convolved(wf, future_taps(k, r))


def first_outer_kernel(side, rim_odd, rim_even, rows_in_odd, rows_in_even, past, future, before, after, hid, act,
                       d1_in, d2_in, bsum, wp, wf, bias, active_in, pre_in,
                       active_out, pre_out, grads, d1, d2):
    frames, rows, chan, _ = active_out.shape
    past_corner, future_corner = corners(side, frames, rows_in_odd, rows_in_even, rim_odd, rim_even)
    past_taps = field(past, before, None, past_corner)
    future_taps = field(future, None, after, future_corner)
    shift = column(bias[...])
    total = bsum[...]
    pres, acts, winp, winf = [], [], [], []
    for f in range(frames):
        for s, r in enumerate((0, rows - 1)):
            winp.append(past_taps(f, r))
            winf.append(future_taps(f, r))
            hidden = convolved(wp, winp[-1]) + shift if f < 2 else hid[f - frames + 2, s]
            grad_act = act[f, s] if f < 2 else convolved(wf, winf[-1])
            active, pre = gated(hidden, grad_act)
            active_out[f, r] = active
            pre_out[f, r] = pre
            acts.append(column_taps(active))
            pres.append(column_taps(pre))
            total = total + pre.astype(F32)
        for r in range(1, rows - 1):
            active_out[f, r] = active_in[f, r]
            pre_out[f, r] = pre_in[f, r]
    bias_sum = jnp.sum(total, axis=1, keepdims=True)
    lanes = lambda parts: jnp.concatenate(parts, axis=1)
    d1[...] = d1_in[...] + lax.dot_general(lanes(pres), lanes(winp), NT, preferred_element_type=F32)
    d2[...] = d2_in[...] + lax.dot_general(lanes(winf), lanes(acts), NT, preferred_element_type=F32)
    per = chan // grads.shape[1]
    for t in range(3):
        for i in range(3):
            for j in range(3):
                left, top = (t * 3 + i) * chan, (8 - t * 3 - i) * chan
                one = d1[j * chan : (j + 1) * chan, left : left + chan]
                two = d2[top : top + chan, (2 - j) * chan : (3 - j) * chan]
                tap = (t * 9 + i * 3 + j) * per
                both = jnp.concatenate([one, two], axis=1).astype(grads.dtype)
                grads[tap : tap + per] = both.reshape((per,) + grads.shape[1:])
    used = 27 * per
    bias_rows = jnp.broadcast_to(bias_sum, (chan, grads.shape[2])).astype(grads.dtype)
    grads[used : used + per] = bias_rows.reshape((per,) + grads.shape[1:])
    rest = grads.shape[0] - used - per
    if rest:
        grads[used + per :] = jnp.zeros((rest,) + grads.shape[1:], grads.dtype)


def second_inner_kernel(side, past, future, rows_odd, rows_even, main_odd, main_even, wp, wf, add_past, add_future,
                        out_past, out_future, before, after):
    frames, rows, _, _ = past.shape
    pick_main(side, main_odd, main_even, before, after)
    past_corner, future_corner = corners(side, frames, rows_odd, rows_even)
    past_taps = field(past, before, None, past_corner)
    future_taps = field(future, None, after, future_corner)
    for f in range(frames):
        for r in range(rows):
            inner = 0 < r < rows - 1
            if f >= 2 or inner:
                out_past[f, r] = (add_past[f, r].astype(F32) + convolved(wp, past_taps(f, r))).astype(BF16)
            if f < frames - 2 or inner:
                out_future[f, r] = (add_future[f, r].astype(F32) + convolved(wf, future_taps(f, r))).astype(BF16)


def second_outer_kernel(side, rim_odd, rim_even, past, future, rows_odd, rows_even, before, after, wp, wf,
                        add_past, add_future, past_in, future_in, out_past, out_future):
    frames, rows, _, _ = out_past.shape
    past_corner, future_corner = corners(side, frames, rows_odd, rows_even, rim_odd, rim_even)
    past_taps = field(past, before, None, past_corner)
    future_taps = field(future, None, after, future_corner)
    for f in range(2):
        for r in (0, rows - 1):
            g = frames - 2 + f
            out_past[f, r] = (add_past[f, r].astype(F32) + convolved(wp, past_taps(f, r))).astype(BF16)
            out_future[g, r] = (add_future[g, r].astype(F32) + convolved(wf, future_taps(g, r))).astype(BF16)
    for f in range(frames):
        for r in range(rows):
            inner = 0 < r < rows - 1
            if f >= 2 or inner:
                out_past[f, r] = past_in[f, r]
            if f < frames - 2 or inner:
                out_future[f, r] = future_in[f, r]


def sum_kernel(parts, out, *, scale):
    lanes = 8
    sums = [parts[k].astype(F32) for k in range(lanes)]
    for k in range(lanes, parts.shape[0]):
        sums[k % lanes] = sums[k % lanes] + parts[k].astype(F32)
    while len(sums) > 1:
        sums = [a + b for a, b in zip(sums[::2], sums[1::2])]
    out[...] = jnp.broadcast_to((sums[0] * scale).astype(out.dtype)[None], out.shape)


def unpack_kernel(parts, one, two, bias):
    taps, chan = one.shape[0], one.shape[1]
    per = chan // parts.shape[1]
    for k in range(taps):
        both = parts[k * per : (k + 1) * per].astype(F32).reshape((chan, 2 * chan))
        one[k] = both[:, :chan]
        two[k] = both[:, chan:]
    column = parts[taps * per : (taps + 1) * per].astype(F32).reshape((chan, 2 * chan))[:, :chan]
    keep = lax.broadcasted_iota(jnp.int32, column.shape, 0) == lax.broadcasted_iota(jnp.int32, column.shape, 1)
    bias[...] = jnp.sum(jnp.where(keep, column, 0.0), axis=0, keepdims=True)


def sides():
    return lax.axis_index("rows") % 2, lax.axis_index("frames") % 2


def call(kernel, outs, args, flops, scratch=(), sided=True):
    vmem = pl.BlockSpec(memory_space=pltpu.VMEM)
    moved = sum(x.size * x.dtype.itemsize for x in list(args) + list(outs))
    body = (lambda *refs: kernel(sides(), *refs)) if sided else kernel
    return pl.pallas_call(
        body,
        out_shape=outs,
        in_specs=[vmem] * len(args),
        out_specs=[vmem] * len(outs),
        scratch_shapes=scratch,
        compiler_params=pltpu.CompilerParams(vmem_limit_bytes=VMEM_LIMIT),
        cost_estimate=pl.CostEstimate(flops=flops, bytes_accessed=moved, transcendentals=0),
    )(*args)


VMEM_LIMIT = 24 * 1024 * 1024


def arrays(*shapes, kind=BF16):
    return [jax.ShapeDtypeStruct(shape, kind) for shape in shapes]


def flat_weights(one, two):
    chan = one.shape[3]
    taps = (27, chan, chan)
    outs = arrays(*[(3 * chan, 9 * chan)] * 4)
    return call(weights_kernel, outs, (one.reshape(taps), two.reshape(taps)), 0, sided=False)


def conv_flops(shape, rows):
    return 2 * 27 * shape[2] * shape[2] * shape[3] * rows


def frame_pair(shape):
    return (2,) + shape[1:]


def first_inner(past, future, main, wp, wf, bias):
    shape = past.shape
    chan, cols = shape[2:]
    outs = arrays(shape, shape, frame_pair(shape), frame_pair(shape)) + arrays(
        (3 * chan, 9 * chan), (9 * chan, 3 * chan), (chan, cols), kind=F32)
    return call(first_inner_kernel, outs, (past, future, *main, wp, wf, bias), conv_flops(shape, 32))


def first_middle(past, future, rows, wp, wf, bias):
    part = (2, 2) + past.shape[2:]
    return call(first_middle_kernel, arrays(part, part, kind=F32), (past, future, *rows, wp, wf, bias),
                conv_flops(past.shape, 8))


def first_outer(devices, past, future, rows, rims, inner, middle, wp, wf, bias):
    active, pre, before, after, *sums = inner
    _, _, chan, _ = active.shape
    outs = arrays(active.shape, pre.shape, (devices, 16, 2 * chan))
    scratch = [pltpu.VMEM((3 * chan, 9 * chan), F32), pltpu.VMEM((9 * chan, 3 * chan), F32)]
    args = (*rims, *rows, past, future, before, after, *middle, *sums, wp, wf, bias, active, pre)
    return call(first_outer_kernel, outs, args, conv_flops(active.shape, 24), scratch)


def second_inner(past, future, rows, main, wp, wf, add_past, add_future):
    shape = past.shape
    outs = arrays(shape, shape, frame_pair(shape), frame_pair(shape))
    args = (past, future, *rows, *main, wp, wf, add_past, add_future)
    return call(second_inner_kernel, outs, args, conv_flops(shape, 24))


def second_outer(past, future, rows, rims, inner, wp, wf, add_past, add_future):
    out_past, out_future, before, after = inner
    args = (*rims, past, future, *rows, before, after, wp, wf, add_past, add_future, out_past, out_future)
    return call(second_outer_kernel, arrays(out_past.shape, out_past.shape), args, conv_flops(out_past.shape, 8))


def repack(past, future):
    frames, _, chan, cols = past.shape
    ends = (2, frames, chan, cols)
    outs = arrays(ends, ends, frame_pair(past.shape), frame_pair(past.shape))
    return call(repack_kernel, outs, (past, future), 0)


def rims_to_send(rows_odd, rows_even):
    rims = (2, 2) + rows_odd.shape[-2:]
    return call(rims_kernel, arrays(rims, rims), (rows_odd, rows_even), 0)


def summed(parts, scale):
    kernel = functools.partial(sum_kernel, scale=scale)
    return call(kernel, arrays(parts.shape), (parts,), 0, sided=False)[0]


def unpacked(parts, chan):
    outs = arrays((27, chan, chan), (27, chan, chan), (1, chan), kind=F32)
    return call(unpack_kernel, outs, (parts,), 0, sided=False)


AXES = ("frames", "rows")


def pairs_of(count, first):
    pairs = []
    for i in range(first, count - 1, 2):
        pairs += [(i, i + 1), (i + 1, i)]
    return pairs


def swap(axis, odd, even):
    count = lax.axis_size(axis)
    even = lax.ppermute(even, axis, pairs_of(count, 0))
    return lax.ppermute(odd, axis, pairs_of(count, 1)), even


def per_device(clip_in, kernel_one, bias_one, kernel_two, cotangent):
    frame_count, row_count, channels, col_count = clip_in.shape
    devices = lax.axis_size("frames") * lax.axis_size("rows")
    cell_total = (
        frame_count * lax.axis_size("frames") * row_count * lax.axis_size("rows") * col_count
    )
    row_even, frame_even = (side == 0 for side in sides())
    both = jnp.stack([clip_in, cotangent])
    first_row, last_row = both[:, :, :1], both[:, :, -1:]
    rows = swap(
        "rows", jnp.where(row_even, first_row, last_row), jnp.where(row_even, last_row, first_row)
    )
    past, future = clip_in[-2:], cotangent[:2]
    main = swap("frames", jnp.where(frame_even, future, past), jnp.where(frame_even, past, future))
    one_fwd, one_adj, two_fwd, two_adj = flat_weights(kernel_one, kernel_two)
    bias = bias_one[None]
    inner = first_inner(clip_in, cotangent, main, one_fwd, two_adj, bias)
    *rows, _ = lax.optimization_barrier((*rows, inner[-1]))
    rims = swap("frames", *rims_to_send(*rows))
    middle = first_middle(clip_in, cotangent, rows, one_fwd, two_adj, bias)
    active, grad_pre, terms = first_outer(
        devices, clip_in, cotangent, rows, rims, inner, middle, one_fwd, two_adj, bias
    )

    terms = lax.all_to_all(terms, AXES, 0, 0, tiled=True)
    spread = summed(terms, 1.0 / math.sqrt(cell_total))
    total = lax.all_to_all(spread, AXES, 0, 0, tiled=True)

    rows_odd, rows_even, main_odd, main_even = repack(active, grad_pre)
    rows = swap("rows", rows_odd, rows_even)
    main = swap("frames", main_odd, main_even)
    *rows, _ = lax.optimization_barrier((*rows, spread))
    rims = swap("frames", *rims_to_send(*rows))
    inner = second_inner(active, grad_pre, rows, main, two_fwd, one_adj, clip_in, cotangent)
    block_out, grad_input = second_outer(
        active, grad_pre, rows, rims, inner, two_fwd, one_adj, clip_in, cotangent
    )
    first, second, bias = unpacked(total, channels)
    return (
        block_out,
        grad_input,
        first.reshape(kernel_one.shape),
        second.reshape(kernel_two.shape),
        bias.reshape(bias_one.shape),
    )


def solution(mesh):
    in_specs = (P("frames", "rows", None, None), P(), P(), P(), P("frames", "rows", None, None))
    out_specs = (P("frames", "rows", None, None), P("frames", "rows", None, None), P(), P(), P())
    return jax.shard_map(per_device, mesh=mesh, in_specs=in_specs, out_specs=out_specs, check_vma=False)
```

```python
import functools
import math

import jax
import jax.numpy as jnp
from jax import lax
from jax.experimental import pallas as pl
from jax.experimental.pallas import tpu as pltpu
from jax.sharding import PartitionSpec as P

F32, BF16 = jnp.float32, jnp.bfloat16
NT = (((1,), (1,)), ((), ()))


def shifted(value, by):
    cols = value.shape[1]
    lane = lax.broadcasted_iota(jnp.int32, value.shape, 1)
    outside = lane == (0 if by == 1 else cols - 1)
    return jnp.where(outside, jnp.zeros_like(value), pltpu.roll(value, by % cols, 1))


def convolved(w, taps):
    part = jnp.dot(w[...], taps, preferred_element_type=F32)
    chan = w.shape[0] // 3
    return shifted(part[:chan], 1) + part[chan : 2 * chan] + shifted(part[2 * chan :], -1)


def column_taps(value):
    return jnp.concatenate([shifted(value, -1), value, shifted(value, 1)], axis=0)


def slab_of(ref, *at):
    return ref[at + (0,) * (len(ref.shape) - 2 - len(at))]


def picker(even, odd_ref, even_ref, swapped):
    one, two = (even_ref, odd_ref) if swapped else (odd_ref, even_ref)
    return lambda *at: jnp.where(even, slab_of(one, *at), slab_of(two, *at))


def field(own, before, after, corner):
    frames, rows, _, cols = own.shape

    def rows_of(g, low, high):
        first = 0 if before is None else before.shape[0]
        if g < first:
            return before[g, low:high]
        if g < first + frames:
            return own[g - first, low:high]
        return after[g - first - frames, low:high]

    def taps(f, r):
        pieces = []
        for g in range(f, f + 3):
            if r == 0:
                pieces.append(corner(g, 0))
            pieces.append(rows_of(g, max(r - 1, 0), min(r + 2, rows)).reshape((-1, cols)))
            if r == rows - 1:
                pieces.append(corner(g, 1))
        return jnp.concatenate(pieces, axis=0)

    return taps


def corners(side, frames, rows_odd, rows_even, rim_odd=None, rim_even=None):
    low = picker(side[0] == 0, rows_odd, rows_even, False)
    high = picker(side[0] == 0, rows_odd, rows_even, True)
    past_rim = picker(side[1] == 0, rim_odd, rim_even, False)
    future_rim = picker(side[1] == 0, rim_odd, rim_even, True)
    past = lambda g, s: past_rim(g, s) if g < 2 else (low, high)[s](0, g - 2)
    future = lambda g, s: future_rim(g - frames, s) if g >= frames else (low, high)[s](1, g)
    return past, future


def pick_main(side, main_odd, main_even, before, after):
    even = side[1] == 0
    past = picker(even, main_odd, main_even, False)
    future = picker(even, main_odd, main_even, True)
    for f in range(before.shape[0]):
        for r in range(before.shape[1]):
            before[f, r] = past(f, r)
            after[f, r] = future(f, r)


def gated(hidden, grad_act):
    sig = jax.nn.sigmoid(hidden)
    return (hidden * sig).astype(BF16), (grad_act * sig * (1.0 + hidden * (1.0 - sig))).astype(BF16)


def repack_kernel(side, past, future, rows_odd, rows_even, main_odd, main_even):
    frames, rows = past.shape[0], past.shape[1]
    row_even, frame_even = side[0] == 0, side[1] == 0
    for f in range(frames):
        for k, src in enumerate((past, future)):
            low, high = src[f, 0], src[f, rows - 1]
            rows_odd[k, f] = jnp.where(row_even, low, high)
            rows_even[k, f] = jnp.where(row_even, high, low)
    for f in range(2):
        for r in range(rows):
            last, first = past[f + frames - 2, r], future[f, r]
            main_odd[f, r] = jnp.where(frame_even, first, last)
            main_even[f, r] = jnp.where(frame_even, last, first)


def rims_kernel(side, rows_odd, rows_even, odd, even):
    frame_even = side[1] == 0
    last = rows_odd.shape[1] - 2
    low = picker(side[0] == 0, rows_odd, rows_even, False)
    high = picker(side[0] == 0, rows_odd, rows_even, True)
    for f in range(2):
        for s, rim in enumerate((low, high)):
            past, future = rim(0, f + last), rim(1, f)
            odd[f, s] = jnp.where(frame_even, future, past)
            even[f, s] = jnp.where(frame_even, past, future)


def weights_kernel(one, two, bias, one_fwd, one_adj, two_fwd, two_adj, bias_out):
    bias_out[...] = column(bias[...])
    chan = one.shape[1]
    for src, fwd, adj in ((one, one_fwd, one_adj), (two, two_fwd, two_adj)):
        for t in range(3):
            for i in range(3):
                for j in range(3):
                    tap = src[t * 9 + i * 3 + j]
                    left = (t * 3 + i) * chan
                    fwd[j * chan : (j + 1) * chan, left : left + chan] = tap
                    left = (8 - t * 3 - i) * chan
                    flipped = jnp.transpose(tap.astype(F32)).astype(BF16)
                    adj[(2 - j) * chan : (3 - j) * chan, left : left + chan] = flipped


def column(row):
    n = row.shape[1]
    spread = jnp.broadcast_to(row, (n, n))
    keep = lax.broadcasted_iota(jnp.int32, (n, n), 0) == lax.broadcasted_iota(jnp.int32, (n, n), 1)
    return jnp.sum(jnp.where(keep, spread, 0.0), axis=1, keepdims=True)


def first_inner_kernel(side, past, future, rows_odd, rows_even, main_odd, main_even, wp, wf, bias,
                       active_out, pre_out, before, after, hid, act, d1, d2, bsum):
    frames, rows, chan, cols = past.shape
    pick_main(side, main_odd, main_even, before, after)
    past_corner, future_corner = corners(side, frames, rows_odd, rows_even)
    past_taps = field(past, before, None, past_corner)
    future_taps = field(future, None, after, future_corner)
    shift = bias[...]
    total = jnp.zeros((chan, cols), F32)
    pres, acts, winp, winf = [], [], [], []
    for f in range(frames):
        for r in range(1, rows - 1):
            winp.append(past_taps(f, r))
            winf.append(future_taps(f, r))
            active, pre = gated(convolved(wp, winp[-1]) + shift, convolved(wf, winf[-1]))
            active_out[f, r] = active
            pre_out[f, r] = pre
            acts.append(column_taps(active))
            pres.append(column_taps(pre))
            total = total + pre.astype(F32)
    for k in range(2):
        for s, r in enumerate((0, rows - 1)):
            hid[k, s] = convolved(wp, past_taps(frames - 2 + k, r)) + shift
            act[k, s] = convolved(wf, future_taps(k, r))
    bsum[...] = total
    lanes = lambda parts: jnp.concatenate(parts, axis=1)
    d1[...] = lax.dot_general(lanes(pres), lanes(winp), NT, preferred_element_type=F32)
    d2[...] = lax.dot_general(lanes(winf), lanes(acts), NT, preferred_element_type=F32)


def first_outer_kernel(side, rim_odd, rim_even, rows_in_odd, rows_in_even, past, future, before, after, hid, act,
                       d1_in, d2_in, bsum, wp, wf, bias, active_in, pre_in,
                       active_out, pre_out, grads, d1, d2):
    frames, rows, chan, _ = active_out.shape
    past_corner, future_corner = corners(side, frames, rows_in_odd, rows_in_even, rim_odd, rim_even)
    past_taps = field(past, before, None, past_corner)
    future_taps = field(future, None, after, future_corner)
    shift = bias[...]
    total = bsum[...]
    pres, acts, winp, winf = [], [], [], []
    for f in range(frames):
        for s, r in enumerate((0, rows - 1)):
            winp.append(past_taps(f, r))
            winf.append(future_taps(f, r))
            hidden = convolved(wp, winp[-1]) + shift if f < 2 else hid[f - frames + 2, s]
            grad_act = act[f, s] if f < 2 else convolved(wf, winf[-1])
            active, pre = gated(hidden, grad_act)
            active_out[f, r] = active
            pre_out[f, r] = pre
            acts.append(column_taps(active))
            pres.append(column_taps(pre))
            total = total + pre.astype(F32)
        for r in range(1, rows - 1):
            active_out[f, r] = active_in[f, r]
            pre_out[f, r] = pre_in[f, r]
    bias_sum = jnp.sum(total, axis=1, keepdims=True)
    lanes = lambda parts: jnp.concatenate(parts, axis=1)
    d1[...] = d1_in[...] + lax.dot_general(lanes(pres), lanes(winp), NT, preferred_element_type=F32)
    d2[...] = d2_in[...] + lax.dot_general(lanes(winf), lanes(acts), NT, preferred_element_type=F32)
    per = chan // grads.shape[1]
    for t in range(3):
        for i in range(3):
            for j in range(3):
                left, top = (t * 3 + i) * chan, (8 - t * 3 - i) * chan
                one = d1[j * chan : (j + 1) * chan, left : left + chan]
                two = d2[top : top + chan, (2 - j) * chan : (3 - j) * chan]
                tap = (t * 9 + i * 3 + j) * per
                both = jnp.concatenate([one, two], axis=1).astype(grads.dtype)
                grads[tap : tap + per] = both.reshape((per,) + grads.shape[1:])
    used = 27 * per
    bias_rows = jnp.broadcast_to(bias_sum, (chan, grads.shape[2])).astype(grads.dtype)
    grads[used : used + per] = bias_rows.reshape((per,) + grads.shape[1:])
    rest = grads.shape[0] - used - per
    if rest:
        grads[used + per :] = jnp.zeros((rest,) + grads.shape[1:], grads.dtype)


def second_inner_kernel(side, past, future, rows_odd, rows_even, main_odd, main_even, wp, wf, add_past, add_future,
                        out_past, out_future, before, after):
    frames, rows, _, _ = past.shape
    pick_main(side, main_odd, main_even, before, after)
    past_corner, future_corner = corners(side, frames, rows_odd, rows_even)
    past_taps = field(past, before, None, past_corner)
    future_taps = field(future, None, after, future_corner)
    for f in range(frames):
        for r in range(rows):
            inner = 0 < r < rows - 1
            if f >= 2 or inner:
                out_past[f, r] = (add_past[f, r].astype(F32) + convolved(wp, past_taps(f, r))).astype(BF16)
            if f < frames - 2 or inner:
                out_future[f, r] = (add_future[f, r].astype(F32) + convolved(wf, future_taps(f, r))).astype(BF16)


def second_outer_kernel(side, rim_odd, rim_even, past, future, rows_odd, rows_even, before, after, wp, wf,
                        add_past, add_future, past_in, future_in, out_past, out_future):
    frames, rows, _, _ = out_past.shape
    past_corner, future_corner = corners(side, frames, rows_odd, rows_even, rim_odd, rim_even)
    past_taps = field(past, before, None, past_corner)
    future_taps = field(future, None, after, future_corner)
    for f in range(2):
        for r in (0, rows - 1):
            g = frames - 2 + f
            out_past[f, r] = (add_past[f, r].astype(F32) + convolved(wp, past_taps(f, r))).astype(BF16)
            out_future[g, r] = (add_future[g, r].astype(F32) + convolved(wf, future_taps(g, r))).astype(BF16)
    for f in range(frames):
        for r in range(rows):
            inner = 0 < r < rows - 1
            if f >= 2 or inner:
                out_past[f, r] = past_in[f, r]
            if f < frames - 2 or inner:
                out_future[f, r] = future_in[f, r]


def sum_kernel(parts, out, *, scale):
    lanes = 8
    sums = [parts[k].astype(F32) for k in range(lanes)]
    for k in range(lanes, parts.shape[0]):
        sums[k % lanes] = sums[k % lanes] + parts[k].astype(F32)
    while len(sums) > 1:
        sums = [a + b for a, b in zip(sums[::2], sums[1::2])]
    out[...] = jnp.broadcast_to((sums[0] * scale).astype(out.dtype)[None], out.shape)


def unpack_kernel(parts, one, two, bias):
    taps, chan = one.shape[0], one.shape[1]
    per = chan // parts.shape[1]
    for k in range(taps):
        both = parts[k * per : (k + 1) * per].astype(F32).reshape((chan, 2 * chan))
        one[k] = both[:, :chan]
        two[k] = both[:, chan:]
    column = parts[taps * per : (taps + 1) * per].astype(F32).reshape((chan, 2 * chan))[:, :chan]
    keep = lax.broadcasted_iota(jnp.int32, column.shape, 0) == lax.broadcasted_iota(jnp.int32, column.shape, 1)
    bias[...] = jnp.sum(jnp.where(keep, column, 0.0), axis=0, keepdims=True)


def sides():
    return lax.axis_index("rows") % 2, lax.axis_index("frames") % 2


def call(kernel, outs, args, flops, scratch=(), sided=True):
    vmem = pl.BlockSpec(memory_space=pltpu.VMEM)
    moved = sum(x.size * x.dtype.itemsize for x in list(args) + list(outs))
    body = (lambda *refs: kernel(sides(), *refs)) if sided else kernel
    return pl.pallas_call(
        body,
        out_shape=outs,
        in_specs=[vmem] * len(args),
        out_specs=[vmem] * len(outs),
        scratch_shapes=scratch,
        compiler_params=pltpu.CompilerParams(vmem_limit_bytes=VMEM_LIMIT),
        cost_estimate=pl.CostEstimate(flops=flops, bytes_accessed=moved, transcendentals=0),
    )(*args)


VMEM_LIMIT = 24 * 1024 * 1024


def arrays(*shapes, kind=BF16):
    return [jax.ShapeDtypeStruct(shape, kind) for shape in shapes]


def flat_weights(one, two, bias):
    chan = one.shape[3]
    taps = (27, chan, chan)
    outs = arrays(*[(3 * chan, 9 * chan)] * 4) + arrays((chan, 1), kind=F32)
    return call(weights_kernel, outs, (one.reshape(taps), two.reshape(taps), bias[None]), 0, sided=False)


def conv_flops(shape, rows):
    return 2 * 27 * shape[2] * shape[2] * shape[3] * rows


def frame_pair(shape):
    return (2,) + shape[1:]


def first_inner(past, future, rows, main, wp, wf, bias):
    shape = past.shape
    chan, cols = shape[2:]
    part = (2, 2, chan, cols)
    outs = arrays(shape, shape, frame_pair(shape), frame_pair(shape)) + arrays(
        part, part, (3 * chan, 9 * chan), (9 * chan, 3 * chan), (chan, cols), kind=F32)
    return call(first_inner_kernel, outs, (past, future, *rows, *main, wp, wf, bias), conv_flops(shape, 40))


def first_outer(devices, past, future, rows, rims, inner, wp, wf, bias):
    active, pre, before, after, *sums = inner
    _, _, chan, _ = active.shape
    outs = arrays(active.shape, pre.shape, (devices, 16, 2 * chan))
    scratch = [pltpu.VMEM((3 * chan, 9 * chan), F32), pltpu.VMEM((9 * chan, 3 * chan), F32)]
    args = (*rims, *rows, past, future, before, after, *sums, wp, wf, bias, active, pre)
    return call(first_outer_kernel, outs, args, conv_flops(active.shape, 24), scratch)


def second_inner(past, future, rows, main, wp, wf, add_past, add_future):
    shape = past.shape
    outs = arrays(shape, shape, frame_pair(shape), frame_pair(shape))
    args = (past, future, *rows, *main, wp, wf, add_past, add_future)
    return call(second_inner_kernel, outs, args, conv_flops(shape, 24))


def second_outer(past, future, rows, rims, inner, wp, wf, add_past, add_future):
    out_past, out_future, before, after = inner
    args = (*rims, past, future, *rows, before, after, wp, wf, add_past, add_future, out_past, out_future)
    return call(second_outer_kernel, arrays(out_past.shape, out_past.shape), args, conv_flops(out_past.shape, 8))


def repack(past, future):
    frames, _, chan, cols = past.shape
    ends = (2, frames, chan, cols)
    outs = arrays(ends, ends, frame_pair(past.shape), frame_pair(past.shape))
    return call(repack_kernel, outs, (past, future), 0)


def rims_to_send(rows_odd, rows_even):
    rims = (2, 2) + rows_odd.shape[-2:]
    return call(rims_kernel, arrays(rims, rims), (rows_odd, rows_even), 0)


def summed(parts, scale):
    kernel = functools.partial(sum_kernel, scale=scale)
    return call(kernel, arrays(parts.shape), (parts,), 0, sided=False)[0]


def unpacked(parts, chan):
    outs = arrays((27, chan, chan), (27, chan, chan), (1, chan), kind=F32)
    return call(unpack_kernel, outs, (parts,), 0, sided=False)


AXES = ("frames", "rows")


def pairs_of(count, first):
    pairs = []
    for i in range(first, count - 1, 2):
        pairs += [(i, i + 1), (i + 1, i)]
    return pairs


def swap(axis, odd, even):
    count = lax.axis_size(axis)
    even = lax.ppermute(even, axis, pairs_of(count, 0))
    return lax.ppermute(odd, axis, pairs_of(count, 1)), even


def per_device(clip_in, kernel_one, bias_one, kernel_two, cotangent):
    frame_count, row_count, channels, col_count = clip_in.shape
    devices = lax.axis_size("frames") * lax.axis_size("rows")
    cell_total = (
        frame_count * lax.axis_size("frames") * row_count * lax.axis_size("rows") * col_count
    )
    row_even, frame_even = (side == 0 for side in sides())
    both = jnp.stack([clip_in, cotangent])
    first_row, last_row = both[:, :, :1], both[:, :, -1:]
    rows = swap(
        "rows", jnp.where(row_even, first_row, last_row), jnp.where(row_even, last_row, first_row)
    )
    past, future = clip_in[-2:], cotangent[:2]
    main = swap("frames", jnp.where(frame_even, future, past), jnp.where(frame_even, past, future))
    one_fwd, one_adj, two_fwd, two_adj, bias = flat_weights(kernel_one, kernel_two, bias_one)
    rims = swap("frames", *rims_to_send(*rows))
    inner = first_inner(clip_in, cotangent, rows, main, one_fwd, two_adj, bias)
    active, grad_pre, terms = first_outer(
        devices, clip_in, cotangent, rows, rims, inner, one_fwd, two_adj, bias
    )

    terms = lax.all_to_all(terms, AXES, 0, 0, tiled=True)
    spread = summed(terms, 1.0 / math.sqrt(cell_total))
    total = lax.all_to_all(spread, AXES, 0, 0, tiled=True)

    rows_odd, rows_even, main_odd, main_even = repack(active, grad_pre)
    rows = swap("rows", rows_odd, rows_even)
    main = swap("frames", main_odd, main_even)
    *rows, _ = lax.optimization_barrier((*rows, spread))
    rims = swap("frames", *rims_to_send(*rows))
    inner = second_inner(active, grad_pre, rows, main, two_fwd, one_adj, clip_in, cotangent)
    block_out, grad_input = second_outer(
        active, grad_pre, rows, rims, inner, two_fwd, one_adj, clip_in, cotangent
    )
    first, second, bias = unpacked(total, channels)
    return (
        block_out,
        grad_input,
        first.reshape(kernel_one.shape),
        second.reshape(kernel_two.shape),
        bias.reshape(bias_one.shape),
    )


def solution(mesh):
    in_specs = (P("frames", "rows", None, None), P(), P(), P(), P("frames", "rows", None, None))
    out_specs = (P("frames", "rows", None, None), P("frames", "rows", None, None), P(), P(), P())
    return jax.shard_map(per_device, mesh=mesh, in_specs=in_specs, out_specs=out_specs, check_vma=False)
```

```python
import functools
import math

import jax
import jax.numpy as jnp
from jax import lax
from jax.experimental import pallas as pl
from jax.experimental.pallas import tpu as pltpu
from jax.sharding import PartitionSpec as P

F32, BF16 = jnp.float32, jnp.bfloat16
NT = (((1,), (1,)), ((), ()))


def shifted(value, by):
    cols = value.shape[1]
    lane = lax.broadcasted_iota(jnp.int32, value.shape, 1)
    outside = lane == (0 if by == 1 else cols - 1)
    return jnp.where(outside, jnp.zeros_like(value), pltpu.roll(value, by % cols, 1))


def convolved(w, taps):
    part = jnp.dot(w[...], taps, preferred_element_type=F32)
    chan = w.shape[0] // 3
    return shifted(part[:chan], 1) + part[chan : 2 * chan] + shifted(part[2 * chan :], -1)


def column_taps(value):
    return jnp.concatenate([shifted(value, -1), value, shifted(value, 1)], axis=0)


def slab_of(ref, *at):
    return ref[at + (0,) * (len(ref.shape) - 2 - len(at))]


def picker(even, odd_ref, even_ref, swapped):
    one, two = (even_ref, odd_ref) if swapped else (odd_ref, even_ref)
    return lambda *at: jnp.where(even, slab_of(one, *at), slab_of(two, *at))


def whole(ref):
    return lambda f, low, high: [ref[f, low:high].reshape((-1, ref.shape[3]))]


def parted(side, k, inner, rows_odd, rows_even):
    count = inner.shape[1] + 2
    first = picker(side[0] == 0, rows_odd, rows_even, False)
    last = picker(side[0] == 0, rows_odd, rows_even, True)

    def rows(f, low, high):
        pieces = [first(k, f)] if low == 0 else []
        pieces.append(inner[f, max(low, 1) - 1 : min(high, count - 1) - 1].reshape((-1, inner.shape[3])))
        return pieces + [last(k, f)] if high == count else pieces

    return rows


def field(own, frames, rows, before, after, corner):
    first = 0 if before is None else before.shape[0]

    def rows_of(g, low, high):
        if g < first:
            return whole(before)(g, low, high)
        if g < first + frames:
            return own(g - first, low, high)
        return whole(after)(g - first - frames, low, high)

    def taps(f, r):
        pieces = []
        for g in range(f, f + 3):
            if r == 0:
                pieces.append(corner(g, 0))
            pieces += rows_of(g, max(r - 1, 0), min(r + 2, rows))
            if r == rows - 1:
                pieces.append(corner(g, 1))
        return jnp.concatenate(pieces, axis=0)

    return taps


def corners(side, frames, rows_odd, rows_even, rim_odd=None, rim_even=None):
    low = picker(side[0] == 0, rows_odd, rows_even, False)
    high = picker(side[0] == 0, rows_odd, rows_even, True)
    past_rim = picker(side[1] == 0, rim_odd, rim_even, False)
    future_rim = picker(side[1] == 0, rim_odd, rim_even, True)
    past = lambda g, s: past_rim(g, s) if g < 2 else (low, high)[s](0, g - 2)
    future = lambda g, s: future_rim(g - frames, s) if g >= frames else (low, high)[s](1, g)
    return past, future


def pick_main(side, main_odd, main_even, before, after):
    even = side[1] == 0
    past = picker(even, main_odd, main_even, False)
    future = picker(even, main_odd, main_even, True)
    for f in range(before.shape[0]):
        for r in range(before.shape[1]):
            before[f, r] = past(f, r)
            after[f, r] = future(f, r)


def gated(hidden, grad_act):
    sig = jax.nn.sigmoid(hidden)
    return (hidden * sig).astype(BF16), (grad_act * sig * (1.0 + hidden * (1.0 - sig))).astype(BF16)


def frames_kernel(side, active, pre, rows_odd, rows_even, main_odd, main_even):
    frame_even = side[1] == 0
    frames, rows = active.shape[0], active.shape[1] + 2
    past = parted(side, 0, active, rows_odd, rows_even)
    future = parted(side, 1, pre, rows_odd, rows_even)
    for f in range(2):
        last = jnp.concatenate(past(f + frames - 2, 0, rows), axis=0)
        first = jnp.concatenate(future(f, 0, rows), axis=0)
        main_odd[f] = jnp.where(frame_even, first, last).reshape(main_odd.shape[1:])
        main_even[f] = jnp.where(frame_even, last, first).reshape(main_even.shape[1:])


def rims_kernel(side, rows_odd, rows_even, odd, even):
    frame_even = side[1] == 0
    last = rows_odd.shape[1] - 2
    low = picker(side[0] == 0, rows_odd, rows_even, False)
    high = picker(side[0] == 0, rows_odd, rows_even, True)
    for f in range(2):
        for s, rim in enumerate((low, high)):
            past, future = rim(0, f + last), rim(1, f)
            odd[f, s] = jnp.where(frame_even, future, past)
            even[f, s] = jnp.where(frame_even, past, future)


def weights_kernel(one, two, bias, one_fwd, one_adj, two_fwd, two_adj, bias_out):
    bias_out[...] = column(bias[...])
    chan = one.shape[1]
    for src, fwd, adj in ((one, one_fwd, one_adj), (two, two_fwd, two_adj)):
        for t in range(3):
            for i in range(3):
                for j in range(3):
                    tap = src[t * 9 + i * 3 + j]
                    left = (t * 3 + i) * chan
                    fwd[j * chan : (j + 1) * chan, left : left + chan] = tap
                    left = (8 - t * 3 - i) * chan
                    flipped = jnp.transpose(tap.astype(F32)).astype(BF16)
                    adj[(2 - j) * chan : (3 - j) * chan, left : left + chan] = flipped


def column(row):
    n = row.shape[1]
    spread = jnp.broadcast_to(row, (n, n))
    keep = lax.broadcasted_iota(jnp.int32, (n, n), 0) == lax.broadcasted_iota(jnp.int32, (n, n), 1)
    return jnp.sum(jnp.where(keep, spread, 0.0), axis=1, keepdims=True)


def first_inner_kernel(side, past, future, rows_odd, rows_even, main_odd, main_even, wp, wf, bias,
                       active_out, pre_out, before, after, hid, act, d1, d2, bsum):
    frames, rows, chan, cols = past.shape
    pick_main(side, main_odd, main_even, before, after)
    past_corner, future_corner = corners(side, frames, rows_odd, rows_even)
    past_taps = field(whole(past), frames, rows, before, None, past_corner)
    future_taps = field(whole(future), frames, rows, None, after, future_corner)
    shift = bias[...]
    total = jnp.zeros((chan, cols), F32)
    pres, acts, winp, winf = [], [], [], []
    for f in range(frames):
        for r in range(1, rows - 1):
            winp.append(past_taps(f, r))
            winf.append(future_taps(f, r))
            active, pre = gated(convolved(wp, winp[-1]) + shift, convolved(wf, winf[-1]))
            active_out[f, r - 1] = active
            pre_out[f, r - 1] = pre
            acts.append(column_taps(active))
            pres.append(column_taps(pre))
            total = total + pre.astype(F32)
    for k in range(2):
        for s, r in enumerate((0, rows - 1)):
            hid[k, s] = convolved(wp, past_taps(frames - 2 + k, r)) + shift
            act[k, s] = convolved(wf, future_taps(k, r))
    bsum[...] = total
    lanes = lambda parts: jnp.concatenate(parts, axis=1)
    d1[...] = lax.dot_general(lanes(pres), lanes(winp), NT, preferred_element_type=F32)
    d2[...] = lax.dot_general(lanes(winf), lanes(acts), NT, preferred_element_type=F32)


def first_outer_kernel(side, rim_odd, rim_even, rows_in_odd, rows_in_even, past, future, before, after, hid, act,
                       d1_in, d2_in, bsum, wp, wf, bias, rows_odd, rows_even, grads, d1, d2):
    frames, rows, chan, _ = past.shape
    row_even = side[0] == 0
    past_corner, future_corner = corners(side, frames, rows_in_odd, rows_in_even, rim_odd, rim_even)
    past_taps = field(whole(past), frames, rows, before, None, past_corner)
    future_taps = field(whole(future), frames, rows, None, after, future_corner)
    shift = bias[...]
    total = bsum[...]
    pres, acts, winp, winf = [], [], [], []
    for f in range(frames):
        ends = []
        for s, r in enumerate((0, rows - 1)):
            winp.append(past_taps(f, r))
            winf.append(future_taps(f, r))
            hidden = convolved(wp, winp[-1]) + shift if f < 2 else hid[f - frames + 2, s]
            grad_act = act[f, s] if f < 2 else convolved(wf, winf[-1])
            active, pre = gated(hidden, grad_act)
            ends.append((active, pre))
            acts.append(column_taps(active))
            pres.append(column_taps(pre))
            total = total + pre.astype(F32)
        for k, (first, last) in enumerate(zip(*ends)):
            rows_odd[k, f] = jnp.where(row_even, first, last)
            rows_even[k, f] = jnp.where(row_even, last, first)
    bias_sum = jnp.sum(total, axis=1, keepdims=True)
    lanes = lambda parts: jnp.concatenate(parts, axis=1)
    d1[...] = d1_in[...] + lax.dot_general(lanes(pres), lanes(winp), NT, preferred_element_type=F32)
    d2[...] = d2_in[...] + lax.dot_general(lanes(winf), lanes(acts), NT, preferred_element_type=F32)
    per = chan // grads.shape[1]
    for t in range(3):
        for i in range(3):
            for j in range(3):
                left, top = (t * 3 + i) * chan, (8 - t * 3 - i) * chan
                one = d1[j * chan : (j + 1) * chan, left : left + chan]
                two = d2[top : top + chan, (2 - j) * chan : (3 - j) * chan]
                tap = (t * 9 + i * 3 + j) * per
                both = jnp.concatenate([one, two], axis=1).astype(grads.dtype)
                grads[tap : tap + per] = both.reshape((per,) + grads.shape[1:])
    used = 27 * per
    bias_rows = jnp.broadcast_to(bias_sum, (chan, grads.shape[2])).astype(grads.dtype)
    grads[used : used + per] = bias_rows.reshape((per,) + grads.shape[1:])
    rest = grads.shape[0] - used - per
    if rest:
        grads[used + per :] = jnp.zeros((rest,) + grads.shape[1:], grads.dtype)


def second_fields(side, active, pre, sent, rows, before, after, rims=(None, None)):
    frames, count = active.shape[0], active.shape[1] + 2
    past_corner, future_corner = corners(side, frames, *rows, *rims)
    past = field(parted(side, 0, active, *sent), frames, count, before, None, past_corner)
    return past, field(parted(side, 1, pre, *sent), frames, count, None, after, future_corner)


def second_inner_kernel(side, active, pre, sent_odd, sent_even, rows_odd, rows_even, main_odd, main_even, wp, wf,
                        add_past, add_future, out_past, out_future, before, after):
    frames, rows, _, _ = out_past.shape
    pick_main(side, main_odd, main_even, before, after)
    past_taps, future_taps = second_fields(
        side, active, pre, (sent_odd, sent_even), (rows_odd, rows_even), before, after)
    for f in range(frames):
        for r in range(rows):
            inner = 0 < r < rows - 1
            if f >= 2 or inner:
                out_past[f, r] = (add_past[f, r].astype(F32) + convolved(wp, past_taps(f, r))).astype(BF16)
            if f < frames - 2 or inner:
                out_future[f, r] = (add_future[f, r].astype(F32) + convolved(wf, future_taps(f, r))).astype(BF16)


def second_outer_kernel(side, rim_odd, rim_even, active, pre, sent_odd, sent_even, rows_odd, rows_even, before, after,
                        wp, wf, add_past, add_future, past_in, future_in, out_past, out_future):
    frames, rows, _, _ = out_past.shape
    past_taps, future_taps = second_fields(
        side, active, pre, (sent_odd, sent_even), (rows_odd, rows_even), before, after, (rim_odd, rim_even))
    for f in range(2):
        for r in (0, rows - 1):
            g = frames - 2 + f
            out_past[f, r] = (add_past[f, r].astype(F32) + convolved(wp, past_taps(f, r))).astype(BF16)
            out_future[g, r] = (add_future[g, r].astype(F32) + convolved(wf, future_taps(g, r))).astype(BF16)
    for f in range(frames):
        for r in range(rows):
            inner = 0 < r < rows - 1
            if f >= 2 or inner:
                out_past[f, r] = past_in[f, r]
            if f < frames - 2 or inner:
                out_future[f, r] = future_in[f, r]


def sum_kernel(parts, out, *, scale):
    lanes = 8
    sums = [parts[k].astype(F32) for k in range(lanes)]
    for k in range(lanes, parts.shape[0]):
        sums[k % lanes] = sums[k % lanes] + parts[k].astype(F32)
    while len(sums) > 1:
        sums = [a + b for a, b in zip(sums[::2], sums[1::2])]
    out[...] = jnp.broadcast_to((sums[0] * scale).astype(out.dtype)[None], out.shape)


def unpack_kernel(parts, one, two, bias):
    taps, chan = one.shape[0], one.shape[1]
    per = chan // parts.shape[1]
    for k in range(taps):
        both = parts[k * per : (k + 1) * per].astype(F32).reshape((chan, 2 * chan))
        one[k] = both[:, :chan]
        two[k] = both[:, chan:]
    column = parts[taps * per : (taps + 1) * per].astype(F32).reshape((chan, 2 * chan))[:, :chan]
    keep = lax.broadcasted_iota(jnp.int32, column.shape, 0) == lax.broadcasted_iota(jnp.int32, column.shape, 1)
    bias[...] = jnp.sum(jnp.where(keep, column, 0.0), axis=0, keepdims=True)


def sides():
    return lax.axis_index("rows") % 2, lax.axis_index("frames") % 2


def call(kernel, outs, args, flops, scratch=(), sided=True):
    vmem = pl.BlockSpec(memory_space=pltpu.VMEM)
    moved = sum(x.size * x.dtype.itemsize for x in list(args) + list(outs))
    body = (lambda *refs: kernel(sides(), *refs)) if sided else kernel
    return pl.pallas_call(
        body,
        out_shape=outs,
        in_specs=[vmem] * len(args),
        out_specs=[vmem] * len(outs),
        scratch_shapes=scratch,
        compiler_params=pltpu.CompilerParams(vmem_limit_bytes=VMEM_LIMIT),
        cost_estimate=pl.CostEstimate(flops=flops, bytes_accessed=moved, transcendentals=0),
    )(*args)


VMEM_LIMIT = 24 * 1024 * 1024


def arrays(*shapes, kind=BF16):
    return [jax.ShapeDtypeStruct(shape, kind) for shape in shapes]


def flat_weights(one, two, bias):
    chan = one.shape[3]
    taps = (27, chan, chan)
    outs = arrays(*[(3 * chan, 9 * chan)] * 4) + arrays((chan, 1), kind=F32)
    return call(weights_kernel, outs, (one.reshape(taps), two.reshape(taps), bias[None]), 0, sided=False)


def conv_flops(shape, rows):
    return 2 * 27 * shape[2] * shape[2] * shape[3] * rows


def frame_pair(shape):
    return (2,) + shape[1:]


def first_inner(past, future, rows, main, wp, wf, bias):
    frames, count, chan, cols = shape = past.shape
    part, inner = (2, 2, chan, cols), (frames, count - 2, chan, cols)
    outs = arrays(inner, inner, frame_pair(shape), frame_pair(shape)) + arrays(
        part, part, (3 * chan, 9 * chan), (9 * chan, 3 * chan), (chan, cols), kind=F32)
    return call(first_inner_kernel, outs, (past, future, *rows, *main, wp, wf, bias), conv_flops(shape, 40))


def first_outer(devices, past, future, rows, rims, partial, wp, wf, bias):
    frames, _, chan, cols = past.shape
    ends = (2, frames, chan, cols)
    outs = arrays(ends, ends, (devices, 16, 2 * chan))
    scratch = [pltpu.VMEM((3 * chan, 9 * chan), F32), pltpu.VMEM((9 * chan, 3 * chan), F32)]
    args = (*rims, *rows, past, future, *partial, wp, wf, bias)
    return call(first_outer_kernel, outs, args, conv_flops(past.shape, 24), scratch)


def second_inner(active, pre, sent, rows, main, wp, wf, add_past, add_future):
    shape = add_past.shape
    outs = arrays(shape, shape, frame_pair(shape), frame_pair(shape))
    args = (active, pre, *sent, *rows, *main, wp, wf, add_past, add_future)
    return call(second_inner_kernel, outs, args, conv_flops(shape, 24))


def second_outer(active, pre, sent, rows, rims, inner, wp, wf, add_past, add_future):
    out_past, out_future, before, after = inner
    args = (*rims, active, pre, *sent, *rows, before, after, wp, wf, add_past, add_future, out_past, out_future)
    return call(second_outer_kernel, arrays(out_past.shape, out_past.shape), args, conv_flops(out_past.shape, 8))


def frames_to_send(active, pre, rows_odd, rows_even):
    _, inner, chan, cols = active.shape
    pair = (2, inner + 2, chan, cols)
    return call(frames_kernel, arrays(pair, pair), (active, pre, rows_odd, rows_even), 0)


def rims_to_send(rows_odd, rows_even):
    rims = (2, 2) + rows_odd.shape[-2:]
    return call(rims_kernel, arrays(rims, rims), (rows_odd, rows_even), 0)


def summed(parts, scale):
    kernel = functools.partial(sum_kernel, scale=scale)
    return call(kernel, arrays(parts.shape), (parts,), 0, sided=False)[0]


def unpacked(parts, chan):
    outs = arrays((27, chan, chan), (27, chan, chan), (1, chan), kind=F32)
    return call(unpack_kernel, outs, (parts,), 0, sided=False)


AXES = ("frames", "rows")


def pairs_of(count, first):
    pairs = []
    for i in range(first, count - 1, 2):
        pairs += [(i, i + 1), (i + 1, i)]
    return pairs


def swap(axis, odd, even):
    count = lax.axis_size(axis)
    even = lax.ppermute(even, axis, pairs_of(count, 0))
    return lax.ppermute(odd, axis, pairs_of(count, 1)), even


def per_device(clip_in, kernel_one, bias_one, kernel_two, cotangent):
    frame_count, row_count, channels, col_count = clip_in.shape
    devices = lax.axis_size("frames") * lax.axis_size("rows")
    cell_total = (
        frame_count * lax.axis_size("frames") * row_count * lax.axis_size("rows") * col_count
    )
    row_even, frame_even = (side == 0 for side in sides())
    both = jnp.stack([clip_in, cotangent])
    first_row, last_row = both[:, :, :1], both[:, :, -1:]
    rows = swap(
        "rows", jnp.where(row_even, first_row, last_row), jnp.where(row_even, last_row, first_row)
    )
    past, future = clip_in[-2:], cotangent[:2]
    main = swap("frames", jnp.where(frame_even, future, past), jnp.where(frame_even, past, future))
    one_fwd, one_adj, two_fwd, two_adj, bias = flat_weights(kernel_one, kernel_two, bias_one)
    rims = swap("frames", *rims_to_send(*rows))
    active, grad_pre, *partial = first_inner(clip_in, cotangent, rows, main, one_fwd, two_adj, bias)
    *sent, terms = first_outer(devices, clip_in, cotangent, rows, rims, partial, one_fwd, two_adj, bias)

    terms = lax.all_to_all(terms, AXES, 0, 0, tiled=True)
    spread = summed(terms, 1.0 / math.sqrt(cell_total))
    total = lax.all_to_all(spread, AXES, 0, 0, tiled=True)

    rows = swap("rows", *sent)
    main = swap("frames", *frames_to_send(active, grad_pre, *sent))
    *rows, _ = lax.optimization_barrier((*rows, spread))
    rims = swap("frames", *rims_to_send(*rows))
    inner = second_inner(active, grad_pre, sent, rows, main, two_fwd, one_adj, clip_in, cotangent)
    block_out, grad_input = second_outer(
        active, grad_pre, sent, rows, rims, inner, two_fwd, one_adj, clip_in, cotangent
    )
    first, second, bias = unpacked(total, channels)
    return (
        block_out,
        grad_input,
        first.reshape(kernel_one.shape),
        second.reshape(kernel_two.shape),
        bias.reshape(bias_one.shape),
    )


def solution(mesh):
    in_specs = (P("frames", "rows", None, None), P(), P(), P(), P("frames", "rows", None, None))
    out_specs = (P("frames", "rows", None, None), P("frames", "rows", None, None), P(), P(), P())
    return jax.shard_map(per_device, mesh=mesh, in_specs=in_specs, out_specs=out_specs, check_vma=False)
```

```python
import functools
import math

import jax
import jax.numpy as jnp
from jax import lax
from jax.experimental import pallas as pl
from jax.experimental.pallas import tpu as pltpu
from jax.sharding import PartitionSpec as P

F32, BF16 = jnp.float32, jnp.bfloat16
NT = (((1,), (1,)), ((), ()))


def shifted(value, by):
    cols = value.shape[1]
    lane = lax.broadcasted_iota(jnp.int32, value.shape, 1)
    outside = lane == (0 if by == 1 else cols - 1)
    return jnp.where(outside, jnp.zeros_like(value), pltpu.roll(value, by % cols, 1))


def convolved(w, taps):
    part = jnp.dot(w[...], taps, preferred_element_type=F32)
    chan = w.shape[0] // 3
    return shifted(part[:chan], 1) + part[chan : 2 * chan] + shifted(part[2 * chan :], -1)


def column_taps(value):
    return jnp.concatenate([shifted(value, -1), value, shifted(value, 1)], axis=0)


def slab_of(ref, *at):
    return ref[at + (0,) * (len(ref.shape) - 2 - len(at))]


def picker(even, odd_ref, even_ref, swapped):
    one, two = (even_ref, odd_ref) if swapped else (odd_ref, even_ref)
    return lambda *at: jnp.where(even, slab_of(one, *at), slab_of(two, *at))


def whole(ref):
    return lambda f, low, high: [ref[f, low:high].reshape((-1, ref.shape[3]))]


def parted(side, k, inner, rows_odd, rows_even):
    count = inner.shape[1] + 2
    first = picker(side[0] == 0, rows_odd, rows_even, False)
    last = picker(side[0] == 0, rows_odd, rows_even, True)

    def rows(f, low, high):
        pieces = [first(k, f)] if low == 0 else []
        pieces.append(inner[f, max(low, 1) - 1 : min(high, count - 1) - 1].reshape((-1, inner.shape[3])))
        return pieces + [last(k, f)] if high == count else pieces

    return rows


def field(own, frames, rows, before, after, corner):
    first = 0 if before is None else before.shape[0]

    def rows_of(g, low, high):
        if g < first:
            return whole(before)(g, low, high)
        if g < first + frames:
            return own(g - first, low, high)
        return whole(after)(g - first - frames, low, high)

    def taps(f, r):
        pieces = []
        for g in range(f, f + 3):
            if r == 0:
                pieces.append(corner(g, 0))
            pieces += rows_of(g, max(r - 1, 0), min(r + 2, rows))
            if r == rows - 1:
                pieces.append(corner(g, 1))
        return jnp.concatenate(pieces, axis=0)

    return taps


def corners(side, frames, rows_odd, rows_even, rim_odd=None, rim_even=None):
    low = picker(side[0] == 0, rows_odd, rows_even, False)
    high = picker(side[0] == 0, rows_odd, rows_even, True)
    past_rim = picker(side[1] == 0, rim_odd, rim_even, False)
    future_rim = picker(side[1] == 0, rim_odd, rim_even, True)
    past = lambda g, s: past_rim(g, s) if g < 2 else (low, high)[s](0, g - 2)
    future = lambda g, s: future_rim(g - frames, s) if g >= frames else (low, high)[s](1, g)
    return past, future


def pick_main(side, main_odd, main_even, before, after):
    even = side[1] == 0
    past = picker(even, main_odd, main_even, False)
    future = picker(even, main_odd, main_even, True)
    for f in range(before.shape[0]):
        for r in range(before.shape[1]):
            before[f, r] = past(f, r)
            after[f, r] = future(f, r)


def gated(hidden, grad_act):
    sig = jax.nn.sigmoid(hidden)
    return (hidden * sig).astype(BF16), (grad_act * sig * (1.0 + hidden * (1.0 - sig))).astype(BF16)


def frames_kernel(side, active, pre, rows_odd, rows_even, main_odd, main_even):
    frame_even = side[1] == 0
    frames, rows = active.shape[0], active.shape[1] + 2
    past = parted(side, 0, active, rows_odd, rows_even)
    future = parted(side, 1, pre, rows_odd, rows_even)
    for f in range(2):
        last = jnp.concatenate(past(f + frames - 2, 0, rows), axis=0)
        first = jnp.concatenate(future(f, 0, rows), axis=0)
        main_odd[f] = jnp.where(frame_even, first, last).reshape(main_odd.shape[1:])
        main_even[f] = jnp.where(frame_even, last, first).reshape(main_even.shape[1:])


def rims_kernel(side, rows_odd, rows_even, odd, even):
    frame_even = side[1] == 0
    last = rows_odd.shape[1] - 2
    low = picker(side[0] == 0, rows_odd, rows_even, False)
    high = picker(side[0] == 0, rows_odd, rows_even, True)
    for f in range(2):
        for s, rim in enumerate((low, high)):
            past, future = rim(0, f + last), rim(1, f)
            odd[f, s] = jnp.where(frame_even, future, past)
            even[f, s] = jnp.where(frame_even, past, future)


def weights_kernel(one, two, bias, one_fwd, one_adj, two_fwd, two_adj, bias_out):
    bias_out[...] = column(bias[...])
    chan = one.shape[1]
    for src, fwd, adj in ((one, one_fwd, one_adj), (two, two_fwd, two_adj)):
        for t in range(3):
            for i in range(3):
                for j in range(3):
                    tap = src[t * 9 + i * 3 + j]
                    left = (t * 3 + i) * chan
                    fwd[j * chan : (j + 1) * chan, left : left + chan] = tap
                    left = (8 - t * 3 - i) * chan
                    flipped = jnp.transpose(tap.astype(F32)).astype(BF16)
                    adj[(2 - j) * chan : (3 - j) * chan, left : left + chan] = flipped


def column(row):
    n = row.shape[1]
    spread = jnp.broadcast_to(row, (n, n))
    keep = lax.broadcasted_iota(jnp.int32, (n, n), 0) == lax.broadcasted_iota(jnp.int32, (n, n), 1)
    return jnp.sum(jnp.where(keep, spread, 0.0), axis=1, keepdims=True)


def first_local_kernel(past, future, wp, wf, bias, hid, act):
    frames, rows, _, _ = past.shape
    past_taps = field(whole(past), frames, rows, None, None, None)
    future_taps = field(whole(future), frames, rows, None, None, None)
    for k in range(2):
        for r in range(1, rows - 1):
            hid[k, r - 1] = convolved(wp, past_taps(k + frames - 4, r)) + bias[...]
            act[k, r - 1] = convolved(wf, future_taps(k, r))


def first_inner_kernel(side, past, future, rows_odd, rows_even, main_odd, main_even, local_hid, local_act, wp, wf, bias,
                       active_out, pre_out, before, after, hid, act, d1, d2, bsum):
    frames, rows, chan, cols = past.shape
    pick_main(side, main_odd, main_even, before, after)
    past_corner, future_corner = corners(side, frames, rows_odd, rows_even)
    past_taps = field(whole(past), frames, rows, before, None, past_corner)
    future_taps = field(whole(future), frames, rows, None, after, future_corner)
    shift = bias[...]
    total = jnp.zeros((chan, cols), F32)
    pres, acts, winp, winf = [], [], [], []
    for f in range(frames):
        for r in range(1, rows - 1):
            winp.append(past_taps(f, r))
            winf.append(future_taps(f, r))
            hidden = convolved(wp, winp[-1]) + shift if f < 2 else local_hid[f - frames + 2, r - 1]
            grad_act = local_act[f, r - 1] if f < 2 else convolved(wf, winf[-1])
            active, pre = gated(hidden, grad_act)
            active_out[f, r - 1] = active
            pre_out[f, r - 1] = pre
            acts.append(column_taps(active))
            pres.append(column_taps(pre))
            total = total + pre.astype(F32)
    for k in range(2):
        for s, r in enumerate((0, rows - 1)):
            hid[k, s] = convolved(wp, past_taps(frames - 2 + k, r)) + shift
            act[k, s] = convolved(wf, future_taps(k, r))
    bsum[...] = total
    lanes = lambda parts: jnp.concatenate(parts, axis=1)
    d1[...] = lax.dot_general(lanes(pres), lanes(winp), NT, preferred_element_type=F32)
    d2[...] = lax.dot_general(lanes(winf), lanes(acts), NT, preferred_element_type=F32)


def first_outer_kernel(side, rim_odd, rim_even, rows_in_odd, rows_in_even, past, future, before, after, hid, act,
                       d1_in, d2_in, bsum, wp, wf, bias, rows_odd, rows_even, grads, d1, d2):
    frames, rows, chan, _ = past.shape
    row_even = side[0] == 0
    past_corner, future_corner = corners(side, frames, rows_in_odd, rows_in_even, rim_odd, rim_even)
    past_taps = field(whole(past), frames, rows, before, None, past_corner)
    future_taps = field(whole(future), frames, rows, None, after, future_corner)
    shift = bias[...]
    total = bsum[...]
    pres, acts, winp, winf = [], [], [], []
    for f in range(frames):
        ends = []
        for s, r in enumerate((0, rows - 1)):
            winp.append(past_taps(f, r))
            winf.append(future_taps(f, r))
            hidden = convolved(wp, winp[-1]) + shift if f < 2 else hid[f - frames + 2, s]
            grad_act = act[f, s] if f < 2 else convolved(wf, winf[-1])
            active, pre = gated(hidden, grad_act)
            ends.append((active, pre))
            acts.append(column_taps(active))
            pres.append(column_taps(pre))
            total = total + pre.astype(F32)
        for k, (first, last) in enumerate(zip(*ends)):
            rows_odd[k, f] = jnp.where(row_even, first, last)
            rows_even[k, f] = jnp.where(row_even, last, first)
    bias_sum = jnp.sum(total, axis=1, keepdims=True)
    lanes = lambda parts: jnp.concatenate(parts, axis=1)
    d1[...] = d1_in[...] + lax.dot_general(lanes(pres), lanes(winp), NT, preferred_element_type=F32)
    d2[...] = d2_in[...] + lax.dot_general(lanes(winf), lanes(acts), NT, preferred_element_type=F32)
    per = chan // grads.shape[1]
    for t in range(3):
        for i in range(3):
            for j in range(3):
                left, top = (t * 3 + i) * chan, (8 - t * 3 - i) * chan
                one = d1[j * chan : (j + 1) * chan, left : left + chan]
                two = d2[top : top + chan, (2 - j) * chan : (3 - j) * chan]
                tap = (t * 9 + i * 3 + j) * per
                both = jnp.concatenate([one, two], axis=1).astype(grads.dtype)
                grads[tap : tap + per] = both.reshape((per,) + grads.shape[1:])
    used = 27 * per
    bias_rows = jnp.broadcast_to(bias_sum, (chan, grads.shape[2])).astype(grads.dtype)
    grads[used : used + per] = bias_rows.reshape((per,) + grads.shape[1:])
    rest = grads.shape[0] - used - per
    if rest:
        grads[used + per :] = jnp.zeros((rest,) + grads.shape[1:], grads.dtype)


def second_fields(side, active, pre, sent, rows, before, after, rims=(None, None)):
    frames, count = active.shape[0], active.shape[1] + 2
    past_corner, future_corner = corners(side, frames, *rows, *rims)
    past = field(parted(side, 0, active, *sent), frames, count, before, None, past_corner)
    return past, field(parted(side, 1, pre, *sent), frames, count, None, after, future_corner)


def second_inner_kernel(side, active, pre, sent_odd, sent_even, rows_odd, rows_even, main_odd, main_even, wp, wf,
                        add_past, add_future, out_past, out_future, before, after):
    frames, rows, _, _ = out_past.shape
    pick_main(side, main_odd, main_even, before, after)
    past_taps, future_taps = second_fields(
        side, active, pre, (sent_odd, sent_even), (rows_odd, rows_even), before, after)
    for f in range(frames):
        for r in range(rows):
            inner = 0 < r < rows - 1
            if f >= 2 or inner:
                out_past[f, r] = (add_past[f, r].astype(F32) + convolved(wp, past_taps(f, r))).astype(BF16)
            if f < frames - 2 or inner:
                out_future[f, r] = (add_future[f, r].astype(F32) + convolved(wf, future_taps(f, r))).astype(BF16)


def second_outer_kernel(side, rim_odd, rim_even, active, pre, sent_odd, sent_even, rows_odd, rows_even, before, after,
                        wp, wf, add_past, add_future, past_in, future_in, out_past, out_future):
    frames, rows, _, _ = out_past.shape
    past_taps, future_taps = second_fields(
        side, active, pre, (sent_odd, sent_even), (rows_odd, rows_even), before, after, (rim_odd, rim_even))
    for f in range(2):
        for r in (0, rows - 1):
            g = frames - 2 + f
            out_past[f, r] = (add_past[f, r].astype(F32) + convolved(wp, past_taps(f, r))).astype(BF16)
            out_future[g, r] = (add_future[g, r].astype(F32) + convolved(wf, future_taps(g, r))).astype(BF16)
    for f in range(frames):
        for r in range(rows):
            inner = 0 < r < rows - 1
            if f >= 2 or inner:
                out_past[f, r] = past_in[f, r]
            if f < frames - 2 or inner:
                out_future[f, r] = future_in[f, r]


def sum_kernel(parts, out, *, scale):
    lanes = 8
    sums = [parts[k].astype(F32) for k in range(lanes)]
    for k in range(lanes, parts.shape[0]):
        sums[k % lanes] = sums[k % lanes] + parts[k].astype(F32)
    while len(sums) > 1:
        sums = [a + b for a, b in zip(sums[::2], sums[1::2])]
    out[...] = jnp.broadcast_to((sums[0] * scale).astype(out.dtype)[None], out.shape)


def unpack_kernel(parts, one_out, two_out, bias, one, two, sems):
    taps, chan = one.shape[0], one.shape[1]
    per = chan // parts.shape[1]
    third = taps // 3
    copies = []
    for t in range(3):
        group = pl.ds(t * third, third)
        for k in range(t * third, (t + 1) * third):
            both = parts[k * per : (k + 1) * per].astype(F32).reshape((chan, 2 * chan))
            one[k] = both[:, :chan]
            two[k] = both[:, chan:]
        for s, (src, dst) in enumerate(((one, one_out), (two, two_out))):
            copies.append(pltpu.make_async_copy(src.at[group], dst.at[group], sems.at[t, s]))
            copies[-1].start()
    column = parts[taps * per : (taps + 1) * per].astype(F32).reshape((chan, 2 * chan))[:, :chan]
    keep = lax.broadcasted_iota(jnp.int32, column.shape, 0) == lax.broadcasted_iota(jnp.int32, column.shape, 1)
    bias[...] = jnp.sum(jnp.where(keep, column, 0.0), axis=0, keepdims=True)
    for copy in copies:
        copy.wait()


def sides():
    return lax.axis_index("rows") % 2, lax.axis_index("frames") % 2


def call(kernel, outs, args, flops, scratch=(), sided=True, copied=0):
    vmem = pl.BlockSpec(memory_space=pltpu.VMEM)
    moved = sum(x.size * x.dtype.itemsize for x in list(args) + list(outs))
    body = (lambda *refs: kernel(sides(), *refs)) if sided else kernel
    return pl.pallas_call(
        body,
        out_shape=outs,
        in_specs=[vmem] * len(args),
        out_specs=[pl.BlockSpec(memory_space=pl.ANY)] * copied + [vmem] * (len(outs) - copied),
        scratch_shapes=scratch,
        compiler_params=pltpu.CompilerParams(vmem_limit_bytes=VMEM_LIMIT),
        cost_estimate=pl.CostEstimate(flops=flops, bytes_accessed=moved, transcendentals=0),
    )(*args)


VMEM_LIMIT = 24 * 1024 * 1024


def arrays(*shapes, kind=BF16):
    return [jax.ShapeDtypeStruct(shape, kind) for shape in shapes]


def flat_weights(one, two, bias):
    chan = one.shape[3]
    taps = (27, chan, chan)
    outs = arrays(*[(3 * chan, 9 * chan)] * 4) + arrays((chan, 1), kind=F32)
    return call(weights_kernel, outs, (one.reshape(taps), two.reshape(taps), bias[None]), 0, sided=False)


def conv_flops(shape, rows):
    return 2 * 27 * shape[2] * shape[2] * shape[3] * rows


def frame_pair(shape):
    return (2,) + shape[1:]


def first_local(past, future, wp, wf, bias):
    _, count, chan, cols = past.shape
    part = (2, count - 2, chan, cols)
    args = (past, future, wp, wf, bias)
    return call(first_local_kernel, arrays(part, part, kind=F32), args, conv_flops(past.shape, 8), sided=False)


def first_inner(past, future, rows, main, local, wp, wf, bias):
    frames, count, chan, cols = shape = past.shape
    part, inner = (2, 2, chan, cols), (frames, count - 2, chan, cols)
    outs = arrays(inner, inner, frame_pair(shape), frame_pair(shape)) + arrays(
        part, part, (3 * chan, 9 * chan), (9 * chan, 3 * chan), (chan, cols), kind=F32)
    return call(first_inner_kernel, outs, (past, future, *rows, *main, *local, wp, wf, bias), conv_flops(shape, 32))


def first_outer(devices, past, future, rows, rims, partial, wp, wf, bias):
    frames, _, chan, cols = past.shape
    ends = (2, frames, chan, cols)
    outs = arrays(ends, ends, (devices, 16, 2 * chan))
    scratch = [pltpu.VMEM((3 * chan, 9 * chan), F32), pltpu.VMEM((9 * chan, 3 * chan), F32)]
    args = (*rims, *rows, past, future, *partial, wp, wf, bias)
    return call(first_outer_kernel, outs, args, conv_flops(past.shape, 24), scratch)


def second_inner(active, pre, sent, rows, main, wp, wf, add_past, add_future):
    shape = add_past.shape
    outs = arrays(shape, shape, frame_pair(shape), frame_pair(shape))
    args = (active, pre, *sent, *rows, *main, wp, wf, add_past, add_future)
    return call(second_inner_kernel, outs, args, conv_flops(shape, 24))


def second_outer(active, pre, sent, rows, rims, inner, wp, wf, add_past, add_future):
    out_past, out_future, before, after = inner
    args = (*rims, active, pre, *sent, *rows, before, after, wp, wf, add_past, add_future, out_past, out_future)
    return call(second_outer_kernel, arrays(out_past.shape, out_past.shape), args, conv_flops(out_past.shape, 8))


def frames_to_send(active, pre, rows_odd, rows_even):
    _, inner, chan, cols = active.shape
    pair = (2, inner + 2, chan, cols)
    return call(frames_kernel, arrays(pair, pair), (active, pre, rows_odd, rows_even), 0)


def rims_to_send(rows_odd, rows_even):
    rims = (2, 2) + rows_odd.shape[-2:]
    return call(rims_kernel, arrays(rims, rims), (rows_odd, rows_even), 0)


def summed(parts, scale):
    kernel = functools.partial(sum_kernel, scale=scale)
    return call(kernel, arrays(parts.shape), (parts,), 0, sided=False)[0]


def unpacked(parts, chan):
    outs = arrays((27, chan, chan), (27, chan, chan), (1, chan), kind=F32)
    scratch = [pltpu.VMEM((27, chan, chan), F32)] * 2 + [pltpu.SemaphoreType.DMA((3, 2))]
    return call(unpack_kernel, outs, (parts,), 0, scratch, sided=False, copied=2)


AXES = ("frames", "rows")


def pairs_of(count, first):
    pairs = []
    for i in range(first, count - 1, 2):
        pairs += [(i, i + 1), (i + 1, i)]
    return pairs


def swap(axis, odd, even):
    count = lax.axis_size(axis)
    even = lax.ppermute(even, axis, pairs_of(count, 0))
    return lax.ppermute(odd, axis, pairs_of(count, 1)), even


def per_device(clip_in, kernel_one, bias_one, kernel_two, cotangent):
    frame_count, row_count, channels, col_count = clip_in.shape
    devices = lax.axis_size("frames") * lax.axis_size("rows")
    cell_total = (
        frame_count * lax.axis_size("frames") * row_count * lax.axis_size("rows") * col_count
    )
    row_even, frame_even = (side == 0 for side in sides())
    both = jnp.stack([clip_in, cotangent])
    first_row, last_row = both[:, :, :1], both[:, :, -1:]
    rows = swap(
        "rows", jnp.where(row_even, first_row, last_row), jnp.where(row_even, last_row, first_row)
    )
    past, future = clip_in[-2:], cotangent[:2]
    main = swap("frames", jnp.where(frame_even, future, past), jnp.where(frame_even, past, future))
    one_fwd, one_adj, two_fwd, two_adj, bias = flat_weights(kernel_one, kernel_two, bias_one)
    local = first_local(clip_in, cotangent, one_fwd, two_adj, bias)
    *rows, _ = lax.optimization_barrier((*rows, local[0]))
    rims = swap("frames", *rims_to_send(*rows))
    active, grad_pre, *partial = first_inner(clip_in, cotangent, rows, main, local, one_fwd, two_adj, bias)
    *sent, terms = first_outer(devices, clip_in, cotangent, rows, rims, partial, one_fwd, two_adj, bias)

    terms = lax.all_to_all(terms, AXES, 0, 0, tiled=True)
    spread = summed(terms, 1.0 / math.sqrt(cell_total))
    total = lax.all_to_all(spread, AXES, 0, 0, tiled=True)

    rows = swap("rows", *sent)
    main = swap("frames", *frames_to_send(active, grad_pre, *sent))
    *rows, _ = lax.optimization_barrier((*rows, spread))
    rims = swap("frames", *rims_to_send(*rows))
    inner = second_inner(active, grad_pre, sent, rows, main, two_fwd, one_adj, clip_in, cotangent)
    block_out, grad_input = second_outer(
        active, grad_pre, sent, rows, rims, inner, two_fwd, one_adj, clip_in, cotangent
    )
    first, second, bias = unpacked(total, channels)
    return (
        block_out,
        grad_input,
        first.reshape(kernel_one.shape),
        second.reshape(kernel_two.shape),
        bias.reshape(bias_one.shape),
    )


def solution(mesh):
    in_specs = (P("frames", "rows", None, None), P(), P(), P(), P("frames", "rows", None, None))
    out_specs = (P("frames", "rows", None, None), P("frames", "rows", None, None), P(), P(), P())
    return jax.shard_map(per_device, mesh=mesh, in_specs=in_specs, out_specs=out_specs, check_vma=False)
```

```python
import functools
import math

import jax
import jax.numpy as jnp
from jax import lax
from jax.experimental import pallas as pl
from jax.experimental.pallas import tpu as pltpu
from jax.sharding import PartitionSpec as P

F32, BF16 = jnp.float32, jnp.bfloat16
NT = (((1,), (1,)), ((), ()))


def shifted(value, by):
    cols = value.shape[1]
    lane = lax.broadcasted_iota(jnp.int32, value.shape, 1)
    outside = lane == (0 if by == 1 else cols - 1)
    return jnp.where(outside, jnp.zeros_like(value), pltpu.roll(value, by % cols, 1))


def convolved(w, taps):
    part = jnp.dot(w[...], taps, preferred_element_type=F32)
    chan = w.shape[0] // 3
    return shifted(part[:chan], 1) + part[chan : 2 * chan] + shifted(part[2 * chan :], -1)


def column_taps(value):
    return jnp.concatenate([shifted(value, -1), value, shifted(value, 1)], axis=0)


def slab_of(ref, *at):
    return ref[at + (0,) * (len(ref.shape) - 2 - len(at))]


def picker(even, odd_ref, even_ref, swapped):
    one, two = (even_ref, odd_ref) if swapped else (odd_ref, even_ref)
    return lambda *at: jnp.where(even, slab_of(one, *at), slab_of(two, *at))


def whole(ref):
    return lambda f, low, high: [ref[f, low:high].reshape((-1, ref.shape[3]))]


def parted(side, k, inner, rows_odd, rows_even):
    count = inner.shape[1] + 2
    first = picker(side[0] == 0, rows_odd, rows_even, False)
    last = picker(side[0] == 0, rows_odd, rows_even, True)

    def rows(f, low, high):
        pieces = [first(k, f)] if low == 0 else []
        pieces.append(inner[f, max(low, 1) - 1 : min(high, count - 1) - 1].reshape((-1, inner.shape[3])))
        return pieces + [last(k, f)] if high == count else pieces

    return rows


def field(own, frames, rows, before, after, corner):
    first = 0 if before is None else before.shape[0]

    def rows_of(g, low, high):
        if g < first:
            return whole(before)(g, low, high)
        if g < first + frames:
            return own(g - first, low, high)
        return whole(after)(g - first - frames, low, high)

    def taps(f, r):
        pieces = []
        for g in range(f, f + 3):
            if r == 0:
                pieces.append(corner(g, 0))
            pieces += rows_of(g, max(r - 1, 0), min(r + 2, rows))
            if r == rows - 1:
                pieces.append(corner(g, 1))
        return jnp.concatenate(pieces, axis=0)

    return taps


def corners(side, frames, rows_odd, rows_even, rim_odd=None, rim_even=None):
    low = picker(side[0] == 0, rows_odd, rows_even, False)
    high = picker(side[0] == 0, rows_odd, rows_even, True)
    past_rim = picker(side[1] == 0, rim_odd, rim_even, False)
    future_rim = picker(side[1] == 0, rim_odd, rim_even, True)
    past = lambda g, s: past_rim(g, s) if g < 2 else (low, high)[s](0, g - 2)
    future = lambda g, s: future_rim(g - frames, s) if g >= frames else (low, high)[s](1, g)
    return past, future


def pick_main(side, main_odd, main_even, before, after):
    even = side[1] == 0
    past = picker(even, main_odd, main_even, False)
    future = picker(even, main_odd, main_even, True)
    for f in range(before.shape[0]):
        for r in range(before.shape[1]):
            before[f, r] = past(f, r)
            after[f, r] = future(f, r)


def gated(hidden, grad_act):
    sig = jax.nn.sigmoid(hidden)
    return (hidden * sig).astype(BF16), (grad_act * sig * (1.0 + hidden * (1.0 - sig))).astype(BF16)


def frames_kernel(side, active, pre, rows_odd, rows_even, main_odd, main_even):
    frame_even = side[1] == 0
    frames, rows = active.shape[0], active.shape[1] + 2
    past = parted(side, 0, active, rows_odd, rows_even)
    future = parted(side, 1, pre, rows_odd, rows_even)
    for f in range(2):
        last = jnp.concatenate(past(f + frames - 2, 0, rows), axis=0)
        first = jnp.concatenate(future(f, 0, rows), axis=0)
        main_odd[f] = jnp.where(frame_even, first, last).reshape(main_odd.shape[1:])
        main_even[f] = jnp.where(frame_even, last, first).reshape(main_even.shape[1:])


def rims_kernel(side, rows_odd, rows_even, odd, even):
    frame_even = side[1] == 0
    last = rows_odd.shape[1] - 2
    low = picker(side[0] == 0, rows_odd, rows_even, False)
    high = picker(side[0] == 0, rows_odd, rows_even, True)
    for f in range(2):
        for s, rim in enumerate((low, high)):
            past, future = rim(0, f + last), rim(1, f)
            odd[f, s] = jnp.where(frame_even, future, past)
            even[f, s] = jnp.where(frame_even, past, future)


def weights_kernel(one, two, bias, one_fwd, one_adj, two_fwd, two_adj, bias_out):
    bias_out[...] = column(bias[...])
    chan = one.shape[1]
    for src, fwd, adj in ((one, one_fwd, one_adj), (two, two_fwd, two_adj)):
        for t in range(3):
            for i in range(3):
                for j in range(3):
                    tap = src[t * 9 + i * 3 + j]
                    left = (t * 3 + i) * chan
                    fwd[j * chan : (j + 1) * chan, left : left + chan] = tap
                    left = (8 - t * 3 - i) * chan
                    flipped = jnp.transpose(tap.astype(F32)).astype(BF16)
                    adj[(2 - j) * chan : (3 - j) * chan, left : left + chan] = flipped


def column(row):
    n = row.shape[1]
    spread = jnp.broadcast_to(row, (n, n))
    keep = lax.broadcasted_iota(jnp.int32, (n, n), 0) == lax.broadcasted_iota(jnp.int32, (n, n), 1)
    return jnp.sum(jnp.where(keep, spread, 0.0), axis=1, keepdims=True)


def first_local_kernel(past, future, wp, wf, bias, hid, act):
    frames, rows, _, _ = past.shape
    past_taps = field(whole(past), frames, rows, None, None, None)
    future_taps = field(whole(future), frames, rows, None, None, None)
    for k in range(2):
        for r in range(1, rows - 1):
            hid[k, r - 1] = convolved(wp, past_taps(k + frames - 4, r)) + bias[...]
            act[k, r - 1] = convolved(wf, future_taps(k, r))


def first_inner_kernel(side, past, future, rows_odd, rows_even, main_odd, main_even, local_hid, local_act, wp, wf, bias,
                       active_out, pre_out, before, after, hid, act, d1, d2, bsum):
    frames, rows, chan, cols = past.shape
    pick_main(side, main_odd, main_even, before, after)
    past_corner, future_corner = corners(side, frames, rows_odd, rows_even)
    past_taps = field(whole(past), frames, rows, before, None, past_corner)
    future_taps = field(whole(future), frames, rows, None, after, future_corner)
    shift = bias[...]
    total = jnp.zeros((chan, cols), F32)
    pres, acts, winp, winf = [], [], [], []
    for f in range(frames):
        for r in range(1, rows - 1):
            winp.append(past_taps(f, r))
            winf.append(future_taps(f, r))
            hidden = convolved(wp, winp[-1]) + shift if f < 2 else local_hid[f - frames + 2, r - 1]
            grad_act = local_act[f, r - 1] if f < 2 else convolved(wf, winf[-1])
            active, pre = gated(hidden, grad_act)
            active_out[f, r - 1] = active
            pre_out[f, r - 1] = pre
            acts.append(column_taps(active))
            pres.append(column_taps(pre))
            total = total + pre.astype(F32)
    for k in range(2):
        for s, r in enumerate((0, rows - 1)):
            hid[k, s] = convolved(wp, past_taps(frames - 2 + k, r)) + shift
            act[k, s] = convolved(wf, future_taps(k, r))
    bsum[...] = total
    lanes = lambda parts: jnp.concatenate(parts, axis=1)
    d1[...] = lax.dot_general(lanes(pres), lanes(winp), NT, preferred_element_type=F32)
    d2[...] = lax.dot_general(lanes(winf), lanes(acts), NT, preferred_element_type=F32)


def first_outer_kernel(side, rim_odd, rim_even, rows_in_odd, rows_in_even, past, future, before, after, hid, act,
                       d1_in, d2_in, bsum, wp, wf, bias, rows_odd, rows_even, grads, d1, d2):
    frames, rows, chan, _ = past.shape
    row_even = side[0] == 0
    past_corner, future_corner = corners(side, frames, rows_in_odd, rows_in_even, rim_odd, rim_even)
    past_taps = field(whole(past), frames, rows, before, None, past_corner)
    future_taps = field(whole(future), frames, rows, None, after, future_corner)
    shift = bias[...]
    total = bsum[...]
    pres, acts, winp, winf = [], [], [], []
    for f in range(frames):
        ends = []
        for s, r in enumerate((0, rows - 1)):
            winp.append(past_taps(f, r))
            winf.append(future_taps(f, r))
            hidden = convolved(wp, winp[-1]) + shift if f < 2 else hid[f - frames + 2, s]
            grad_act = act[f, s] if f < 2 else convolved(wf, winf[-1])
            active, pre = gated(hidden, grad_act)
            ends.append((active, pre))
            acts.append(column_taps(active))
            pres.append(column_taps(pre))
            total = total + pre.astype(F32)
        for k, (first, last) in enumerate(zip(*ends)):
            rows_odd[k, f] = jnp.where(row_even, first, last)
            rows_even[k, f] = jnp.where(row_even, last, first)
    bias_sum = jnp.sum(total, axis=1, keepdims=True)
    lanes = lambda parts: jnp.concatenate(parts, axis=1)
    d1[...] = d1_in[...] + lax.dot_general(lanes(pres), lanes(winp), NT, preferred_element_type=F32)
    d2[...] = d2_in[...] + lax.dot_general(lanes(winf), lanes(acts), NT, preferred_element_type=F32)
    per = chan // grads.shape[1]
    for t in range(3):
        for i in range(3):
            for j in range(3):
                left, top = (t * 3 + i) * chan, (8 - t * 3 - i) * chan
                one = d1[j * chan : (j + 1) * chan, left : left + chan]
                two = d2[top : top + chan, (2 - j) * chan : (3 - j) * chan]
                tap = (t * 9 + i * 3 + j) * per
                both = jnp.concatenate([one, two], axis=1).astype(grads.dtype)
                grads[tap : tap + per] = both.reshape((per,) + grads.shape[1:])
    used = 27 * per
    bias_rows = jnp.broadcast_to(bias_sum, (chan, grads.shape[2])).astype(grads.dtype)
    grads[used : used + per] = bias_rows.reshape((per,) + grads.shape[1:])
    rest = grads.shape[0] - used - per
    if rest:
        grads[used + per :] = jnp.zeros((rest,) + grads.shape[1:], grads.dtype)


def second_fields(side, active, pre, sent, rows, before, after, rims=(None, None)):
    frames, count = active.shape[0], active.shape[1] + 2
    past_corner, future_corner = corners(side, frames, *rows, *rims)
    past = field(parted(side, 0, active, *sent), frames, count, before, None, past_corner)
    return past, field(parted(side, 1, pre, *sent), frames, count, None, after, future_corner)


def second_inner_kernel(side, active, pre, sent_odd, sent_even, rows_odd, rows_even, main_odd, main_even, wp, wf,
                        add_past, add_future, out_past, out_future, before, after):
    frames, rows, _, _ = out_past.shape
    pick_main(side, main_odd, main_even, before, after)
    past_taps, future_taps = second_fields(
        side, active, pre, (sent_odd, sent_even), (rows_odd, rows_even), before, after)
    for f in range(frames):
        for r in range(rows):
            inner = 0 < r < rows - 1
            if f >= 2 or inner:
                out_past[f, r] = (add_past[f, r].astype(F32) + convolved(wp, past_taps(f, r))).astype(BF16)
            if f < frames - 2 or inner:
                out_future[f, r] = (add_future[f, r].astype(F32) + convolved(wf, future_taps(f, r))).astype(BF16)


def second_outer_kernel(side, rim_odd, rim_even, active, pre, sent_odd, sent_even, rows_odd, rows_even, before, after,
                        wp, wf, add_past, add_future, past_in, future_in, out_past, out_future):
    frames, rows, _, _ = out_past.shape
    past_taps, future_taps = second_fields(
        side, active, pre, (sent_odd, sent_even), (rows_odd, rows_even), before, after, (rim_odd, rim_even))
    for f in range(2):
        for r in (0, rows - 1):
            g = frames - 2 + f
            out_past[f, r] = (add_past[f, r].astype(F32) + convolved(wp, past_taps(f, r))).astype(BF16)
            out_future[g, r] = (add_future[g, r].astype(F32) + convolved(wf, future_taps(g, r))).astype(BF16)
    for f in range(frames):
        for r in range(rows):
            inner = 0 < r < rows - 1
            if f >= 2 or inner:
                out_past[f, r] = past_in[f, r]
            if f < frames - 2 or inner:
                out_future[f, r] = future_in[f, r]


def sum_kernel(parts, out, *, scale):
    lanes = 8
    sums = [parts[k].astype(F32) for k in range(lanes)]
    for k in range(lanes, parts.shape[0]):
        sums[k % lanes] = sums[k % lanes] + parts[k].astype(F32)
    while len(sums) > 1:
        sums = [a + b for a, b in zip(sums[::2], sums[1::2])]
    out[...] = jnp.broadcast_to((sums[0] * scale).astype(out.dtype)[None], out.shape)


def unpack_kernel(parts, one, two, bias):
    taps, chan = one.shape[0], one.shape[1]
    per = chan // parts.shape[1]
    for k in range(taps):
        both = parts[k * per : (k + 1) * per].astype(F32).reshape((chan, 2 * chan))
        one[k] = both[:, :chan]
        two[k] = both[:, chan:]
    column = parts[taps * per : (taps + 1) * per].astype(F32).reshape((chan, 2 * chan))[:, :chan]
    keep = lax.broadcasted_iota(jnp.int32, column.shape, 0) == lax.broadcasted_iota(jnp.int32, column.shape, 1)
    bias[...] = jnp.sum(jnp.where(keep, column, 0.0), axis=0, keepdims=True)


def sides():
    return lax.axis_index("rows") % 2, lax.axis_index("frames") % 2


def call(kernel, outs, args, flops, scratch=(), sided=True):
    vmem = pl.BlockSpec(memory_space=pltpu.VMEM)
    moved = sum(x.size * x.dtype.itemsize for x in list(args) + list(outs))
    body = (lambda *refs: kernel(sides(), *refs)) if sided else kernel
    return pl.pallas_call(
        body,
        out_shape=outs,
        in_specs=[vmem] * len(args),
        out_specs=[vmem] * len(outs),
        scratch_shapes=scratch,
        compiler_params=pltpu.CompilerParams(vmem_limit_bytes=VMEM_LIMIT),
        cost_estimate=pl.CostEstimate(flops=flops, bytes_accessed=moved, transcendentals=0),
    )(*args)


VMEM_LIMIT = 24 * 1024 * 1024


def arrays(*shapes, kind=BF16):
    return [jax.ShapeDtypeStruct(shape, kind) for shape in shapes]


def flat_weights(one, two, bias):
    chan = one.shape[3]
    taps = (27, chan, chan)
    outs = arrays(*[(3 * chan, 9 * chan)] * 4) + arrays((chan, 1), kind=F32)
    return call(weights_kernel, outs, (one.reshape(taps), two.reshape(taps), bias[None]), 0, sided=False)


def conv_flops(shape, rows):
    return 2 * 27 * shape[2] * shape[2] * shape[3] * rows


def frame_pair(shape):
    return (2,) + shape[1:]


def first_local(past, future, wp, wf, bias):
    _, count, chan, cols = past.shape
    part = (2, count - 2, chan, cols)
    args = (past, future, wp, wf, bias)
    return call(first_local_kernel, arrays(part, part, kind=F32), args, conv_flops(past.shape, 8), sided=False)


def first_inner(past, future, rows, main, local, wp, wf, bias):
    frames, count, chan, cols = shape = past.shape
    part, inner = (2, 2, chan, cols), (frames, count - 2, chan, cols)
    outs = arrays(inner, inner, frame_pair(shape), frame_pair(shape)) + arrays(
        part, part, (3 * chan, 9 * chan), (9 * chan, 3 * chan), (chan, cols), kind=F32)
    return call(first_inner_kernel, outs, (past, future, *rows, *main, *local, wp, wf, bias), conv_flops(shape, 32))


def first_outer(devices, past, future, rows, rims, partial, wp, wf, bias):
    frames, _, chan, cols = past.shape
    ends = (2, frames, chan, cols)
    outs = arrays(ends, ends, (devices, 16, 2 * chan))
    scratch = [pltpu.VMEM((3 * chan, 9 * chan), F32), pltpu.VMEM((9 * chan, 3 * chan), F32)]
    args = (*rims, *rows, past, future, *partial, wp, wf, bias)
    return call(first_outer_kernel, outs, args, conv_flops(past.shape, 24), scratch)


def second_inner(active, pre, sent, rows, main, wp, wf, add_past, add_future):
    shape = add_past.shape
    outs = arrays(shape, shape, frame_pair(shape), frame_pair(shape))
    args = (active, pre, *sent, *rows, *main, wp, wf, add_past, add_future)
    return call(second_inner_kernel, outs, args, conv_flops(shape, 24))


def second_outer(active, pre, sent, rows, rims, inner, wp, wf, add_past, add_future):
    out_past, out_future, before, after = inner
    args = (*rims, active, pre, *sent, *rows, before, after, wp, wf, add_past, add_future, out_past, out_future)
    return call(second_outer_kernel, arrays(out_past.shape, out_past.shape), args, conv_flops(out_past.shape, 8))


def frames_to_send(active, pre, rows_odd, rows_even):
    _, inner, chan, cols = active.shape
    pair = (2, inner + 2, chan, cols)
    return call(frames_kernel, arrays(pair, pair), (active, pre, rows_odd, rows_even), 0)


def rims_to_send(rows_odd, rows_even):
    rims = (2, 2) + rows_odd.shape[-2:]
    return call(rims_kernel, arrays(rims, rims), (rows_odd, rows_even), 0)


def summed(parts, scale):
    kernel = functools.partial(sum_kernel, scale=scale)
    return call(kernel, arrays(parts.shape), (parts,), 0, sided=False)[0]


def unpacked(parts, chan):
    outs = arrays((27, chan, chan), (27, chan, chan), (1, chan), kind=F32)
    return call(unpack_kernel, outs, (parts,), 0, sided=False)


AXES = ("frames", "rows")


def pairs_of(count, first):
    pairs = []
    for i in range(first, count - 1, 2):
        pairs += [(i, i + 1), (i + 1, i)]
    return pairs


def swap(axis, odd, even):
    count = lax.axis_size(axis)
    even = lax.ppermute(even, axis, pairs_of(count, 0))
    return lax.ppermute(odd, axis, pairs_of(count, 1)), even


def per_device(clip_in, kernel_one, bias_one, kernel_two, cotangent):
    frame_count, row_count, channels, col_count = clip_in.shape
    devices = lax.axis_size("frames") * lax.axis_size("rows")
    cell_total = (
        frame_count * lax.axis_size("frames") * row_count * lax.axis_size("rows") * col_count
    )
    row_side, frame_side = sides()
    frame_even = frame_side == 0
    over_odd = row_side * (row_count - 1)

    def row_of_both(r):
        return jnp.stack([lax.dynamic_slice_in_dim(x, r, 1, axis=1) for x in (clip_in, cotangent)])

    rows = swap("rows", row_of_both(over_odd), row_of_both(row_count - 1 - over_odd))
    past, future = clip_in[-2:], cotangent[:2]
    main = swap("frames", jnp.where(frame_even, future, past), jnp.where(frame_even, past, future))
    one_fwd, one_adj, two_fwd, two_adj, bias = flat_weights(kernel_one, kernel_two, bias_one)
    local = first_local(clip_in, cotangent, one_fwd, two_adj, bias)
    *rows, _ = lax.optimization_barrier((*rows, local[0]))
    rims = swap("frames", *rims_to_send(*rows))
    active, grad_pre, *partial = first_inner(clip_in, cotangent, rows, main, local, one_fwd, two_adj, bias)
    *sent, terms = first_outer(devices, clip_in, cotangent, rows, rims, partial, one_fwd, two_adj, bias)

    terms = lax.all_to_all(terms, AXES, 0, 0, tiled=True)
    spread = summed(terms, 1.0 / math.sqrt(cell_total))
    total = lax.all_to_all(spread, AXES, 0, 0, tiled=True)

    rows = swap("rows", *sent)
    main = swap("frames", *frames_to_send(active, grad_pre, *sent))
    *rows, _ = lax.optimization_barrier((*rows, spread))
    rims = swap("frames", *rims_to_send(*rows))
    inner = second_inner(active, grad_pre, sent, rows, main, two_fwd, one_adj, clip_in, cotangent)
    block_out, grad_input = second_outer(
        active, grad_pre, sent, rows, rims, inner, two_fwd, one_adj, clip_in, cotangent
    )
    first, second, bias = unpacked(total, channels)
    return (
        block_out,
        grad_input,
        first.reshape(kernel_one.shape),
        second.reshape(kernel_two.shape),
        bias.reshape(bias_one.shape),
    )


def solution(mesh):
    in_specs = (P("frames", "rows", None, None), P(), P(), P(), P("frames", "rows", None, None))
    out_specs = (P("frames", "rows", None, None), P("frames", "rows", None, None), P(), P(), P())
    return jax.shard_map(per_device, mesh=mesh, in_specs=in_specs, out_specs=out_specs, check_vma=False)
```
